128 devices in a mesh: row: 16 (over z, x), col: 8 (over y, core).
Axes of the slice: x: 4, y: 4, z: 4, core: 2. Of those that a mesh axis runs over, the one named last changes fastest.
Arguments:
- leaf_mass: bfloat16 [128, 2048, 2048], P(('row', 'col')), as said below
- tile_mask: int32 [128, 16, 16], P(('row', 'col')), may hold values from 0 to 1, as said below
- constraint_modes: bfloat16 [128, 2048, 1024], P(('row', 'col')), may hold values from -0.125 to 0.125
- leaf_fixed_modes: bfloat16 [128, 2048, 128], P(('row', 'col')), may hold values from -6 to 6
- block_map: int32 [128, 2, 4], P(('row', 'col')), may hold values from 0 to 3, each once within a row
- group_mass: float32 [8, 512, 512], P('col', 'row'), as said below
- top_mass: float32 [512, 512], P(('row', 'col')), as said below
- group_basis: float32 [8, 512, 128], P('col', 'row'), may hold values from -6 to 6
- top_basis: float32 [512, 128], P('row'), may hold values from -6 to 6
Outputs:
- coupling: float32 [128, 128, 2, 128], P(('row', 'col'))
- group_modes: float32 [8, 512, 128], P('col', 'row')
- top_modes: float32 [512, 128], P('row')
- group_assembled: float32 [8, 512, 512], P('col', 'row')
- apex_gathered_mass: float32 [512, 512], P(('row', 'col'))
The draws below stay inside these ranges and needn't reach their ends.
Inputs may be any that keep to these rules, and one draw needn't show every extreme that they name: `tile_mask`: symmetric in its two tile indices, with ones on the diagonal tiles. block_map[l, k] is a permutation of the 4 separator blocks. `leaf_mass`: each leaf's matrix is symmetric and strictly diagonally dominant with a positive diagonal. `group_mass`: each group's matrix is symmetric and strictly diagonally dominant with a positive diagonal. `top_mass`: symmetric and strictly diagonally dominant with a positive diagonal.
All inputs are finite; a program needn't handle non-finite values.
Results may differ from the reference program's by a relative error of at most 0.0029.
Values sent between devices are 32-bit elements; how exact they have to be, the bound alone decides.
A program may use at most 128 MiB of HBM per device.

```python
import jax
import jax.numpy as jnp
from jax import lax

SUBDOMAIN_DOFS = 2048
TILE = 128
SEP = 512
SEP_BLOCK = 128
MODES = 128
LEAVES = 128
GROUPS = 8
TILES = 16
SEPB = 4


def dominant(key, matrix_rows, destination):
    sampled = jax.random.normal(key, (matrix_rows, matrix_rows), jnp.float32)
    symmetric = 0.5 * (sampled + sampled.T)
    off_diagonal_part = symmetric * (1.0 - jnp.eye(matrix_rows, dtype=jnp.float32))
    margin = jax.random.uniform(jax.random.fold_in(key, 7), (matrix_rows,), jnp.float32, 1.2, 2.0)
    diagonal_part = jnp.sum(jnp.abs(off_diagonal_part), axis=1) * margin
    assembled = off_diagonal_part + jnp.diag(diagonal_part)
    return assembled * (destination / jnp.mean(diagonal_part))


def draw_leaf_mass(key, part):
    mass_unit = 1.0 / (LEAVES // GROUPS * SEP)

    def draw_one(leaf_index):
        subdomain_seed = jax.random.fold_in(key, leaf_index)
        rising = 1.0 + 2.0 * leaf_index.astype(jnp.float32) / max(LEAVES - 1, 1)
        scale_row = mass_unit * rising * jax.random.uniform(jax.random.fold_in(subdomain_seed, 1), (SUBDOMAIN_DOFS,), jnp.float32, 0.85, 1.15)
        root_row = jnp.sqrt(scale_row)
        narrow_spread = jnp.diag(scale_row)
        for position, offset in enumerate((1, TILE - 1, TILE, TILE + 1)):
            sub_key = jax.random.fold_in(subdomain_seed, 10 + position)
            weights = jax.random.uniform(sub_key, (SUBDOMAIN_DOFS - offset,), jnp.float32, 0.05, 0.09)
            upper_band = jnp.diag(weights * root_row[:-offset] * root_row[offset:], offset)
            narrow_spread = narrow_spread + upper_band + upper_band.T
        permute_degrees = jax.random.permutation(jax.random.fold_in(subdomain_seed, 2), SUBDOMAIN_DOFS)
        return narrow_spread[permute_degrees][:, permute_degrees].astype(jnp.bfloat16)
    return lax.map(draw_one, jnp.arange(LEAVES, dtype=jnp.int32))


def draw_tile_mask(key, part):
    patch_flags = jax.random.randint(jax.random.fold_in(key, 11), (LEAVES, TILES, TILES), 0, 2, dtype=jnp.int32)
    upper_part = jnp.triu(patch_flags, 1)
    identity_part = jnp.eye(TILES, dtype=jnp.int32)[None, :, :]
    return upper_part + jnp.swapaxes(upper_part, 1, 2) + identity_part


def draw_group_mass(key, part):

    def draw_one(group_index):
        return dominant(jax.random.fold_in(key, group_index + 101), SEP, 0.5 / SEP)
    return lax.map(draw_one, jnp.arange(GROUPS, dtype=jnp.int32))


def draw_top_mass(key, part):
    return dominant(jax.random.fold_in(key, 202), SEP, 0.5 * GROUPS / SEP)


def block_levels(rng, extent, shards, least, top_value):
    level = 1.0
    for dim, shards_of in shards:
        heights = jax.random.uniform(jax.random.fold_in(jax.random.fold_in(rng, 6), dim), (shards_of,), jnp.float32, least / len(shards), top_value / len(shards))
        level = level * jnp.repeat(jnp.exp(heights), extent[dim] // shards_of).reshape((-1,) + (1,) * (len(extent) - 1 - dim))
    return level


def scatter_about(key, dims, scale, most, split=(), held_as=jnp.bfloat16):
    array = jax.random.normal(key, dims, jnp.float32) * scale
    if len(split) > 0:
        array = block_levels(key, dims, split, -0.22, 0.18) * array
    return jnp.clip(array, min=-most, max=most).astype(held_as)


def setup_inputs(seed: int = 0) -> dict:
    streams_of = jax.random.split(jax.random.key(seed), 10)
    leaf_mass = draw_leaf_mass(jax.random.fold_in(streams_of[9], 71), 0)
    tile_mask = draw_tile_mask(jax.random.fold_in(streams_of[9], 71), 0)
    constraint_modes = scatter_about(streams_of[2], (LEAVES, SUBDOMAIN_DOFS, 2 * SEP), SUBDOMAIN_DOFS ** -0.5, 0.125, ((0, 128),))
    leaf_fixed_modes = scatter_about(streams_of[3], (LEAVES, SUBDOMAIN_DOFS, MODES), (((LEAVES // GROUPS) * SEP // SUBDOMAIN_DOFS) ** 0.5), 6.0, ((0, 128),))
    block_map = jax.vmap(lambda own: jax.random.permutation(own, SEPB))(jax.random.split(streams_of[4], LEAVES * 2)).reshape((LEAVES, 2, SEPB)).astype(jnp.int32)
    group_mass = draw_group_mass(jax.random.fold_in(streams_of[9], 71), 0)
    top_mass = draw_top_mass(jax.random.fold_in(streams_of[9], 71), 0)
    group_basis = scatter_about(streams_of[7], (GROUPS, SEP, MODES), 1.0, 6.0, ((0, 8), (1, 16)), jnp.float32)
    top_basis = scatter_about(streams_of[8], (SEP, MODES), 1.0, 6.0, ((0, 16),), jnp.float32)
    return {"leaf_mass": leaf_mass, "tile_mask": tile_mask, "constraint_modes": constraint_modes, "leaf_fixed_modes": leaf_fixed_modes, "block_map": block_map, "group_mass": group_mass, "top_mass": top_mass, "group_basis": group_basis, "top_basis": top_basis}


def expand_mask(leaf_matrix, tile_flags):
    tile_count = tile_flags.shape[0]
    leaf_rows = leaf_matrix.shape[0]
    chosen = tile_flags.astype(jnp.bfloat16)
    tiled = leaf_matrix.reshape(tile_count, TILE, tile_count, TILE) * chosen[:, None, :, None]
    return tiled.reshape(leaf_rows, leaf_rows)

def contract_product(left_side, right_side):
    return lax.dot_general(left_side.astype(jnp.float32), right_side.astype(jnp.float32), (((0,), (0,)), ((), ())), preferred_element_type=jnp.float32)

def to_separator(partial_value, ordering):
    block_count = SEP // SEP_BLOCK
    inverse = jnp.argsort(ordering)
    blocks = partial_value.reshape(block_count, SEP_BLOCK, block_count, SEP_BLOCK)
    blocks = blocks[inverse][:, :, inverse]
    return blocks.reshape(SEP, SEP)

def to_leaf(mode_rows, ordering):
    block_count = SEP // SEP_BLOCK
    blocks = mode_rows.reshape(block_count, SEP_BLOCK, mode_rows.shape[1])
    return blocks[ordering].reshape(SEP, mode_rows.shape[1])

def orthonormal(separator_matrix, basis_rows):
    applied = jnp.dot(separator_matrix, basis_rows, precision=lax.Precision.HIGHEST)
    gram_matrix = jnp.dot(basis_rows.T, applied, precision=lax.Precision.HIGHEST)
    gram_matrix = 0.5 * (gram_matrix + gram_matrix.T)
    lower_factor = jnp.linalg.cholesky(gram_matrix)
    return lax.linalg.triangular_solve(lower_factor, basis_rows, left_side=False, lower=True, transpose_a=True)

def reference(leaf_mass, tile_mask, constraint_modes, leaf_fixed_modes, block_map, group_mass, top_mass, group_basis, top_basis):

    def leaf_work(leaf_entries):
        leaf_matrix, tile_flags, modes_c, modes_l, ordering = leaf_entries
        masked = expand_mask(leaf_matrix, tile_flags)
        loaded = jnp.dot(masked.astype(jnp.float32), modes_c.astype(jnp.float32), preferred_element_type=jnp.float32).astype(jnp.bfloat16)
        partial_group = contract_product(modes_c[:, :SEP], loaded[:, :SEP])
        partial_top = contract_product(modes_c[:, SEP:], loaded[:, SEP:])
        projected = contract_product(modes_l, loaded)
        return (to_separator(partial_group, ordering[0]), to_separator(partial_top, ordering[1]), projected)
    sep_group, sep_top, projected = lax.map(leaf_work, (leaf_mass, tile_mask, constraint_modes, leaf_fixed_modes, block_map))
    group_matrix = group_mass + jnp.sum(sep_group.reshape(LEAVES // GROUPS, GROUPS, SEP, SEP), axis=0)
    top_matrix = top_mass + jnp.sum(sep_top, axis=0)
    group_assembled = SEP * group_matrix
    apex_gathered_mass = SEP * top_matrix
    group_modes = jax.vmap(orthonormal)(group_matrix, group_basis)
    top_modes = orthonormal(top_matrix, top_basis)
    group_index = (jnp.arange(LEAVES) % GROUPS).astype(jnp.int32)

    def couple(leaf_entries):
        leaf_projected, ordering, which_group = leaf_entries
        modes_group = to_leaf(group_modes[which_group], ordering[0])
        modes_top = to_leaf(top_modes, ordering[1])
        first = jnp.dot(leaf_projected[:, :SEP], modes_group, precision=lax.Precision.HIGHEST)
        second = jnp.dot(leaf_projected[:, SEP:], modes_top, precision=lax.Precision.HIGHEST)
        return jnp.stack([first, second], axis=1)
    coupling = lax.map(couple, (projected, block_map, group_index))
    return (coupling, group_modes, top_modes, group_assembled, apex_gathered_mass)
```

```python
import jax
import jax.numpy as jnp
from jax import lax
from jax.experimental import pallas as pl
from jax.experimental.pallas import tpu as pltpu
from jax.sharding import PartitionSpec as P

TILE = 128
SEP = 512
ROWS = 16
COLS = 8
N = 2048
CHUNK = 256
CHUNKS = N // CHUNK
F32 = jnp.float32
BF16 = jnp.bfloat16
MESH = pl.DeviceIdType.MESH
HIGHEST = lax.Precision.HIGHEST


def dot_tn(a, b, **kw):
    return lax.dot_general(a, b, (((0,), (0,)), ((), ())), preferred_element_type=F32, **kw)


def dot_nt(a, b, **kw):
    return lax.dot_general(a, b, (((1,), (1,)), ((), ())), preferred_element_type=F32, **kw)


def dot_nn(a, b, **kw):
    return jnp.dot(a, b, preferred_element_type=F32, **kw)


def split_three(u):
    a = u.astype(BF16).astype(F32)
    rest = u - a
    b = rest.astype(BF16).astype(F32)
    c = rest - b
    return a, b, c


def is_block(value, i):
    top, below = 1, 1
    for j in range(4):
        if j != i:
            top = top * (value - j)
            below = below * (i - j)
    return lax.div(top * (1 if below > 0 else -1), abs(below))


def factor_panel(ch, w, p):
    k = pl.multiple_of(p * 8, 8)
    shift = lax.rem(128 - k, 128)
    sub = lax.broadcasted_iota(jnp.int32, (8, 128), 0)
    for m in range(2):
        pa = ch[m, pl.ds(k, 8), 0:128]
        pw = ch[m, pl.ds(k, 8), 128:256]
        d = pltpu.roll(pa, shift, 1)
        c = [jnp.broadcast_to(d[:, j : j + 1], (8, 128)) for j in range(8)]
        scale = jnp.zeros((8, 128), F32)
        for j in range(8):
            pivot = jnp.broadcast_to(c[j][j : j + 1, :], (8, 128))
            root = lax.rsqrt(pivot)
            scale = jnp.where(sub == j, root, scale)
            if j < 7:
                f = jnp.where(sub > j, c[j] * (root * root), 0.0)
                pa = pa - f * jnp.broadcast_to(pa[j : j + 1, :], (8, 128))
                pw = pw - f * jnp.broadcast_to(pw[j : j + 1, :], (8, 128))
                for q in range(j + 1, 8):
                    c[q] = c[q] - f * jnp.broadcast_to(c[q][j : j + 1, :], (8, 128))
        ua = pa * scale
        uw = pw * scale
        w[m, pl.ds(k, 8), :] = uw
        a1, a2, a3 = split_three(ua)
        w1, w2, w3 = split_three(uw)
        left = jnp.concatenate([a1, a1, a2, a2, a1, a3], axis=0).astype(BF16)
        right = jnp.concatenate(
            [
                jnp.concatenate([a1, a2, a1, a2, a3, a1], axis=0),
                jnp.concatenate([w1, w2, w1, w2, w3, w1], axis=0),
            ],
            axis=1,
        ).astype(BF16)
        ch[m] = ch[m] - dot_tn(left, right)


def kernel(
    mass_hbm,
    mask_ref,
    modes_hbm,
    fixed_hbm,
    map_ref,
    gmass_hbm,
    tmass_hbm,
    gbasis_hbm,
    tbasis_hbm,
    coup_ref,
    gmodes_ref,
    tmodes_ref,
    gout_ref,
    apex_ref,
    raw,
    masked,
    cin,
    cp,
    loaded,
    fixed,
    maskrow,
    gmass,
    tmass,
    xall,
    part,
    gram,
    g_in,
    g_sum,
    g_all,
    t_in,
    t_sum,
    t_row,
    t_fin,
    t_all,
    opp1,
    own1,
    acc1,
    s1,
    opp2,
    own2,
    acc2,
    tcol,
    tcol_in,
    ch,
    winv,
    lsem,
    bsem,
    msem,
    x_send,
    x_recv,
    g1_send,
    g1_recv,
    g2_send,
    g2_recv,
    ta_send,
    ta_recv,
    tb_send,
    tb_recv,
    tc_send,
    tc_recv,
    r_send,
    r_recv,
    k_send,
    k_recv,
):
    r = lax.axis_index("row")
    c = lax.axis_index("col")
    z = lax.div(r, 4)
    x = lax.rem(r, 4)

    locals_ = [
        None,
        pltpu.make_async_copy(fixed_hbm, fixed, lsem.at[1]),
        pltpu.make_async_copy(gmass_hbm, gmass, lsem.at[2]),
        pltpu.make_async_copy(tmass_hbm, tmass, lsem.at[3]),
        pltpu.make_async_copy(gbasis_hbm, xall.at[r, 0], lsem.at[4]),
        pltpu.make_async_copy(tbasis_hbm, xall.at[r, 1], lsem.at[5]),
    ]
    blocks = [
        pltpu.make_async_copy(
            modes_hbm.at[:, pl.ds(b * TILE, TILE)], cin.at[b], bsem.at[b]
        )
        for b in range(8)
    ]
    chunks = [
        pltpu.make_async_copy(
            mass_hbm.at[pl.ds(i * CHUNK, CHUNK)], raw.at[pl.ds(i * CHUNK, CHUNK)], msem.at[i]
        )
        for i in range(CHUNKS)
    ]
    locals_[4].start()
    locals_[5].start()
    for b in range(8):
        blocks[b].start()
    chunks[0].start()
    chunks[1].start()
    locals_[2].start()
    locals_[3].start()
    for i in range(2, CHUNKS):
        chunks[i].start()
    locals_[1].start()

    barrier = pltpu.get_barrier_semaphore()

    @pl.loop(1, ROWS)
    def _(d):
        pl.semaphore_signal(
            barrier, inc=1, device_id=(lax.rem(r + d, ROWS), c), device_id_type=MESH
        )

    @pl.loop(1, COLS)
    def _(d):
        pl.semaphore_signal(
            barrier, inc=1, device_id=(r, lax.rem(c + d, COLS)), device_id_type=MESH
        )

    for b in range(16):
        maskrow[:, b * TILE : (b + 1) * TILE] = jnp.broadcast_to(
            mask_ref[:, b : b + 1].astype(F32), (16, TILE)
        )

    def apply_mask(i):
        chunks[i].wait()
        for half in range(2):
            rows = i * CHUNK + half * TILE
            a = i * 2 + half
            m = jnp.broadcast_to(maskrow[a : a + 1, :], (16, N)).astype(BF16)
            for q in range(TILE // 16):
                masked[i % 2, half * TILE + q * 16 : half * TILE + (q + 1) * 16, :] = (
                    raw[rows + q * 16 : rows + (q + 1) * 16, :] * m
                )

    for b in range(8):
        blocks[b].wait()
    for k in range(2):
        for i in range(4):
            at = 0
            for a in range(1, 4):
                at = at + a * is_block(map_ref[k, a], i)
            to = k * SEP + i * TILE
            cp[:, to : to + TILE] = cin[k * 4 + lax.rem(at, 4)]
    apply_mask(0)

    pl.semaphore_wait(barrier, ROWS - 1 + COLS - 1)
    locals_[4].wait()
    locals_[5].wait()

    def row_copy(d, src, dst, send, recv):
        return pltpu.make_async_remote_copy(
            src_ref=src,
            dst_ref=dst,
            send_sem=send.at[d],
            recv_sem=recv.at[d],
            device_id=(lax.rem(r + d, ROWS), c),
            device_id_type=MESH,
        )

    def col_copy(d, src, dst, send, recv):
        return pltpu.make_async_remote_copy(
            src_ref=src,
            dst_ref=dst,
            send_sem=send.at[d],
            recv_sem=recv.at[d],
            device_id=(r, lax.rem(c + d, COLS)),
            device_id_type=MESH,
        )

    def each_row(fn):
        @pl.loop(1, ROWS)
        def _(d):
            fn(d)

    def each_col(fn):
        @pl.loop(1, COLS)
        def _(d):
            fn(d)

    def src_row(d):
        return lax.rem(r + ROWS - d, ROWS)

    def src_col(d):
        return lax.rem(c + COLS - d, COLS)

    x_copy = lambda d: row_copy(d, xall.at[r], xall.at[r], x_send, x_recv)
    x_wait = lambda d: row_copy(d, xall.at[r], xall.at[src_row(d)], x_send, x_recv)
    each_row(lambda d: x_copy(d).start())

    for i in range(CHUNKS):
        if i + 1 < CHUNKS:
            apply_mask(i + 1)
        loaded[i * CHUNK : (i + 1) * CHUNK, :] = dot_nn(masked[i % 2], cp[...]).astype(BF16)

    each_row(lambda d: x_wait(d).wait_recv())

    part[0] = dot_tn(cp[:, 0:SEP], loaded[:, 0:SEP]).reshape(4, 4, 32, SEP)
    part[1] = dot_tn(cp[:, SEP:], loaded[:, SEP:]).reshape(4, 4, 32, SEP)
    locals_[2].wait()
    locals_[3].wait()
    part[0, z, x] = part[0, z, x] + gmass[...]
    own_rows = lax.div(lax.broadcasted_iota(jnp.int32, (32, SEP), 0), 4) == c
    own_top = jnp.concatenate([tmass[...]] * 8, axis=0)
    part[1, z, x] = part[1, z, x] + jnp.where(own_rows, own_top, 0.0)

    def basis(m):
        return xall[:, m].reshape(SEP, 128)

    for m in (1, 0):
        applied = dot_nn(part[m].reshape(SEP, SEP), basis(m), precision=HIGHEST)
        gram[m] = dot_tn(basis(m), applied, precision=HIGHEST)
        if m == 1:
            for q in range(COLS):
                t_row[q] = gram[1, q * 16 : (q + 1) * 16, :]
            each_col(
                lambda d: col_copy(
                    d, t_row.at[lax.rem(c + d, COLS)], t_in.at[c], ta_send, ta_recv
                ).start()
            )
    for q in range(ROWS):
        g_sum[q] = gram[0, q * 8 : (q + 1) * 8, :]
    each_row(
        lambda d: row_copy(
            d, g_sum.at[lax.rem(r + d, ROWS)], g_in.at[r], g1_send, g1_recv
        ).start()
    )
    t_in[c] = t_row[c]
    g_in[r] = g_sum[r]

    locals_[1].wait()
    projected = dot_tn(fixed[...], loaded[...])
    seen = [
        dot_nn(projected[:, m * SEP : (m + 1) * SEP], basis(m), precision=HIGHEST)
        for m in range(2)
    ]
    coup_ref[:, 0:128] = seen[0]
    coup_ref[:, 128:256] = seen[1]

    each_col(
        lambda d: col_copy(d, t_row.at[0], t_in.at[src_col(d)], ta_send, ta_recv).wait_recv()
    )
    total = t_in[0]
    for q in range(1, COLS):
        total = total + t_in[q]
    t_sum[r] = total
    each_row(lambda d: row_copy(d, t_sum.at[r], t_sum.at[r], tb_send, tb_recv).start())

    each_row(
        lambda d: row_copy(d, g_sum.at[0], g_in.at[src_row(d)], g1_send, g1_recv).wait_recv()
    )
    total = g_in[0]
    for q in range(1, ROWS):
        total = total + g_in[q]
    g_all[r] = total
    each_row(lambda d: row_copy(d, g_all.at[r], g_all.at[r], g2_send, g2_recv).start())

    def ring(phase, arr):
        along_z = (arr == 0) == (phase == 1)
        me = z if along_z else x

        def device(step):
            to = lax.rem(me + step + 4, 4)
            return (to * 4 + x, c) if along_z else (z * 4 + to, c)

        return me, device

    def source(phase, arr, dest, half):
        if phase == 1:
            if arr == 0:
                return part.at[0, dest, pl.ds(half * 2, 2)]
            return part.at[1, pl.ds(half * 2, 2), dest]
        return s1.at[arr, dest, pl.ds(half * 16, 16)]

    boxes = {1: (opp1, own1, acc1), 2: (opp2, own2, acc2)}

    def ring_copy(phase, arr, kind, way, src):
        _, device = ring(phase, arr)
        slot = ((phase - 1) * 2 + arr) * 6 + kind * 2 + way
        return pltpu.make_async_remote_copy(
            src_ref=src,
            dst_ref=boxes[phase][kind].at[arr, way],
            send_sem=r_send.at[slot],
            recv_sem=r_recv.at[slot],
            device_id=device(1 - 2 * way),
            device_id_type=MESH,
        )

    def opp_copy(phase, arr, way):
        me, _ = ring(phase, arr)
        return ring_copy(phase, arr, 0, way, source(phase, arr, lax.rem(me + 2, 4), way))

    def own_copy(phase, arr, way):
        me, _ = ring(phase, arr)
        dest = lax.rem(me + 1 - 2 * way + 4, 4)
        return ring_copy(phase, arr, 1, way, source(phase, arr, dest, 1 - way))

    def acc_copy(phase, arr, way):
        return ring_copy(phase, arr, 2, way, boxes[phase][0].at[arr, way])

    def ring_open(phase):
        for copy in (opp_copy, own_copy):
            for arr in range(2):
                for way in range(2):
                    copy(phase, arr, way).start()

    def ring_pass(phase):
        for arr in range(2):
            me, _ = ring(phase, arr)
            for way in range(2):
                opp_copy(phase, arr, way).wait_recv()
                dest = lax.rem(me + 1 - 2 * way + 4, 4)
                box = boxes[phase][0].at[arr, way]
                box[...] = box[...] + source(phase, arr, dest, way)[...]
                acc_copy(phase, arr, way).start()

    def ring_close(phase, arr):
        me, _ = ring(phase, arr)
        halves = []
        for half in range(2):
            acc_copy(phase, arr, half).wait_recv()
            own_copy(phase, arr, 1 - half).wait_recv()
            halves.append(
                source(phase, arr, me, half)[...]
                + boxes[phase][2][arr, half]
                + boxes[phase][1][arr, 1 - half]
            )
        return halves

    ring_open(1)

    each_row(
        lambda d: row_copy(d, t_sum.at[r], t_sum.at[src_row(d)], tb_send, tb_recv).wait_recv()
    )
    total = t_sum[0]
    for q in range(1, ROWS):
        total = total + t_sum[q]
    t_all[c] = total
    each_col(lambda d: col_copy(d, t_all.at[c], t_all.at[c], tc_send, tc_recv).start())

    each_row(
        lambda d: row_copy(d, g_all.at[r], g_all.at[src_row(d)], g2_send, g2_recv).wait_recv()
    )
    each_col(
        lambda d: col_copy(d, t_all.at[c], t_all.at[src_col(d)], tc_send, tc_recv).wait_recv()
    )
    eye = (
        lax.broadcasted_iota(jnp.int32, (128, 128), 0)
        == lax.broadcasted_iota(jnp.int32, (128, 128), 1)
    ).astype(F32)
    for m, whole in enumerate((g_all[...], t_all[...])):
        whole = whole.reshape(128, 128)
        ch[m, :, 0:128] = 0.5 * (whole + whole.T)
        ch[m, :, 128:256] = eye

    def panels(lo, hi):
        @pl.loop(lo, hi)
        def _(p):
            factor_panel(ch, winv, p)

    panels(0, 3)
    ring_pass(1)
    panels(3, 7)
    for arr in range(2):
        halves = ring_close(1, arr)
        s1[arr, 0:2] = halves[0]
        s1[arr, 2:4] = halves[1]
    ring_open(2)
    panels(7, 10)
    ring_pass(2)
    panels(10, 13)
    halves = ring_close(2, 1)
    for half in range(2):
        for q in range(4):
            tcol[half * 4 + q] = halves[half][q * 4 : (q + 1) * 4, :]
    each_col(
        lambda d: col_copy(
            d, tcol.at[lax.rem(c + d, COLS)], tcol_in.at[c], k_send, k_recv
        ).start()
    )
    tcol_in[c] = tcol[c]
    halves = ring_close(2, 0)
    for half in range(2):
        gout_ref[half * 16 : (half + 1) * 16, :] = SEP * halves[half]
    panels(13, 16)

    first = dot_nt(coup_ref[:, 0:128], winv[0], precision=HIGHEST)
    second = dot_nt(coup_ref[:, 128:256], winv[1], precision=HIGHEST)
    coup_ref[:, 0:128] = first
    coup_ref[:, 128:256] = second
    gmodes_ref[...] = dot_nt(xall[r, 0], winv[0], precision=HIGHEST)
    tmodes_ref[...] = dot_nt(xall[r, 1], winv[1], precision=HIGHEST)

    each_col(
        lambda d: col_copy(d, tcol.at[0], tcol_in.at[src_col(d)], k_send, k_recv).wait_recv()
    )
    total = tcol_in[0]
    for q in range(1, COLS):
        total = total + tcol_in[q]
    apex_ref[...] = SEP * total

    def sends_row(d):
        x_copy(d).wait_send()
        row_copy(d, g_sum.at[0], g_in.at[r], g1_send, g1_recv).wait_send()
        row_copy(d, g_all.at[r], g_all.at[r], g2_send, g2_recv).wait_send()
        row_copy(d, t_sum.at[r], t_sum.at[r], tb_send, tb_recv).wait_send()

    def sends_col(d):
        col_copy(d, t_row.at[0], t_in.at[c], ta_send, ta_recv).wait_send()
        col_copy(d, t_all.at[c], t_all.at[c], tc_send, tc_recv).wait_send()
        col_copy(d, tcol.at[0], tcol_in.at[c], k_send, k_recv).wait_send()

    each_row(sends_row)
    each_col(sends_col)
    for phase in (1, 2):
        for copy in (opp_copy, own_copy, acc_copy):
            for arr in range(2):
                for way in range(2):
                    copy(phase, arr, way).wait_send()


def body(
    leaf_mass,
    tile_mask,
    constraint_modes,
    leaf_fixed_modes,
    block_map,
    group_mass,
    top_mass,
    group_basis,
    top_basis,
):
    hbm = pl.BlockSpec(memory_space=pl.ANY)
    vmem = pl.BlockSpec(memory_space=pltpu.VMEM)
    smem = pl.BlockSpec(memory_space=pltpu.SMEM)
    dma = pltpu.SemaphoreType.DMA
    half1 = (2, 2, 2, 32, SEP)
    half2 = (2, 2, 16, SEP)
    scratch = [
        pltpu.VMEM((N, N), BF16),
        pltpu.VMEM((2, CHUNK, N), BF16),
        pltpu.VMEM((8, N, TILE), BF16),
        pltpu.VMEM((N, 2 * SEP), BF16),
        pltpu.VMEM((N, 2 * SEP), BF16),
        pltpu.VMEM((N, 128), BF16),
        pltpu.VMEM((16, N), F32),
        pltpu.VMEM((32, SEP), F32),
        pltpu.VMEM((4, SEP), F32),
        pltpu.VMEM((ROWS, 2, 32, 128), F32),
        pltpu.VMEM((2, 4, 4, 32, SEP), F32),
        pltpu.VMEM((2, 128, 128), F32),
        pltpu.VMEM((ROWS, 8, 128), F32),
        pltpu.VMEM((ROWS, 8, 128), F32),
        pltpu.VMEM((ROWS, 8, 128), F32),
        pltpu.VMEM((COLS, 16, 128), F32),
        pltpu.VMEM((ROWS, 16, 128), F32),
        pltpu.VMEM((COLS, 16, 128), F32),
        pltpu.VMEM((COLS, 16, 128), F32),
        pltpu.VMEM((COLS, 16, 128), F32),
        pltpu.VMEM(half1, F32),
        pltpu.VMEM(half1, F32),
        pltpu.VMEM(half1, F32),
        pltpu.VMEM((2, 4, 32, SEP), F32),
        pltpu.VMEM(half2, F32),
        pltpu.VMEM(half2, F32),
        pltpu.VMEM(half2, F32),
        pltpu.VMEM((COLS, 4, SEP), F32),
        pltpu.VMEM((COLS, 4, SEP), F32),
        pltpu.VMEM((2, 128, 256), F32),
        pltpu.VMEM((2, 128, 128), F32),
        dma((6,)),
        dma((8,)),
        dma((CHUNKS,)),
        dma((ROWS,)),
        dma((ROWS,)),
        dma((ROWS,)),
        dma((ROWS,)),
        dma((ROWS,)),
        dma((ROWS,)),
        dma((COLS,)),
        dma((COLS,)),
        dma((ROWS,)),
        dma((ROWS,)),
        dma((COLS,)),
        dma((COLS,)),
        dma((24,)),
        dma((24,)),
        dma((COLS,)),
        dma((COLS,)),
    ]
    coupling, gmodes, tmodes, gout, apex = pl.pallas_call(
        kernel,
        out_shape=(
            jax.ShapeDtypeStruct((128, 256), F32),
            jax.ShapeDtypeStruct((32, 128), F32),
            jax.ShapeDtypeStruct((32, 128), F32),
            jax.ShapeDtypeStruct((32, SEP), F32),
            jax.ShapeDtypeStruct((4, SEP), F32),
        ),
        in_specs=[hbm, vmem, hbm, hbm, smem, hbm, hbm, hbm, hbm],
        out_specs=(vmem, vmem, vmem, vmem, vmem),
        scratch_shapes=scratch,
        compiler_params=pltpu.CompilerParams(
            collective_id=0, has_side_effects=True, vmem_limit_bytes=60 << 20
        ),
        name="assemble",
    )(
        leaf_mass[0],
        tile_mask[0],
        constraint_modes[0],
        leaf_fixed_modes[0],
        block_map[0],
        group_mass[0],
        top_mass,
        group_basis[0],
        top_basis,
    )
    return (coupling.reshape(1, 128, 2, 128), gmodes[None], tmodes, gout[None], apex)


def solution(mesh):
    in_specs = (
        P(("row", "col"), None, None),
        P(("row", "col"), None, None),
        P(("row", "col"), None, None),
        P(("row", "col"), None, None),
        P(("row", "col"), None, None),
        P("col", "row", None),
        P(("row", "col"), None),
        P("col", "row", None),
        P("row", None),
    )
    out_specs = (
        P(("row", "col"), None, None, None),
        P("col", "row", None),
        P("row", None),
        P("col", "row", None),
        P(("row", "col"), None),
    )
    return jax.shard_map(body, mesh=mesh, in_specs=in_specs, out_specs=out_specs, check_vma=False)
```

```python
import jax
import jax.numpy as jnp
from jax import lax
from jax.experimental import pallas as pl
from jax.experimental.pallas import tpu as pltpu
from jax.sharding import PartitionSpec as P

TILE = 128
SEP = 512
ROWS = 16
COLS = 8
N = 2048
CHUNK = 1024
CHUNKS = N // CHUNK
F32 = jnp.float32
BF16 = jnp.bfloat16
MESH = pl.DeviceIdType.MESH
HIGHEST = lax.Precision.HIGHEST


def dot_tn(a, b, **kw):
    return lax.dot_general(a, b, (((0,), (0,)), ((), ())), preferred_element_type=F32, **kw)


def dot_nt(a, b, **kw):
    return lax.dot_general(a, b, (((1,), (1,)), ((), ())), preferred_element_type=F32, **kw)


def dot_nn(a, b, **kw):
    return jnp.dot(a, b, preferred_element_type=F32, **kw)


def split_three(u):
    a = u.astype(BF16).astype(F32)
    rest = u - a
    b = rest.astype(BF16).astype(F32)
    c = rest - b
    return a, b, c


def is_block(value, i):
    top, below = 1, 1
    for j in range(4):
        if j != i:
            top = top * (value - j)
            below = below * (i - j)
    return lax.div(top * (1 if below > 0 else -1), abs(below))


def factor_panel(ch, w, p):
    k = p * 8
    sub = lax.broadcasted_iota(jnp.int32, (8, 128), 0)
    for m in range(2):
        pa = ch[m, k : k + 8, 0:128]
        pw = ch[m, k : k + 8, 128:256]
        c = [jnp.broadcast_to(pa[:, k + j : k + j + 1], (8, 128)) for j in range(8)]
        scale = jnp.zeros((8, 128), F32)
        for j in range(8):
            pivot = jnp.broadcast_to(c[j][j : j + 1, :], (8, 128))
            root = lax.rsqrt(pivot)
            scale = jnp.where(sub == j, root, scale)
            if j < 7:
                f = jnp.where(sub > j, c[j] * (root * root), 0.0)
                pa = pa - f * jnp.broadcast_to(pa[j : j + 1, :], (8, 128))
                pw = pw - f * jnp.broadcast_to(pw[j : j + 1, :], (8, 128))
                for q in range(j + 1, 8):
                    c[q] = c[q] - f * jnp.broadcast_to(c[q][j : j + 1, :], (8, 128))
        ua = pa * scale
        uw = pw * scale
        w[m, k : k + 8, :] = uw
        if p == 15:
            continue
        a1, a2, a3 = split_three(ua)
        w1, w2, w3 = split_three(uw)
        left = jnp.concatenate([a1, a1, a2, a2, a1, a3], axis=0).astype(BF16)
        right = jnp.concatenate(
            [
                jnp.concatenate([a1, a2, a1, a2, a3, a1], axis=0),
                jnp.concatenate([w1, w2, w1, w2, w3, w1], axis=0),
            ],
            axis=1,
        ).astype(BF16)
        ch[m, k + 8 :] = ch[m, k + 8 :] - dot_tn(left, right)[k + 8 :]


def split_two(v):
    high = v.astype(BF16)
    return high, (v - high.astype(F32)).astype(BF16)


def kernel(
    mass_hbm,
    mask_ref,
    modes_hbm,
    fixed_hbm,
    map_ref,
    gmass_hbm,
    tmass_hbm,
    gbasis_hbm,
    tbasis_hbm,
    seen_ref,
    w_ref,
    own_ref,
    gout_ref,
    apex_ref,
    raw,
    masked,
    cin,
    cp,
    loaded,
    fixed,
    maskrow,
    gmass,
    tmass,
    xall,
    part,
    gram,
    g_in,
    g_sum,
    g_all,
    t_in,
    t_sum,
    t_row,
    t_fin,
    t_all,
    opp1,
    own1,
    acc1,
    s1,
    opp2,
    own2,
    acc2,
    tcol,
    tcol_in,
    ch,
    lsem,
    bsem,
    msem,
    x_send,
    x_recv,
    g1_send,
    g1_recv,
    g2_send,
    g2_recv,
    ta_send,
    ta_recv,
    tb_send,
    tb_recv,
    tc_send,
    tc_recv,
    r_send,
    r_recv,
    k_send,
    k_recv,
):
    r = lax.axis_index("row")
    c = lax.axis_index("col")
    z = lax.div(r, 4)
    x = lax.rem(r, 4)

    locals_ = [
        None,
        pltpu.make_async_copy(fixed_hbm, fixed, lsem.at[1]),
        pltpu.make_async_copy(gmass_hbm, gmass, lsem.at[2]),
        pltpu.make_async_copy(tmass_hbm, tmass, lsem.at[3]),
        pltpu.make_async_copy(gbasis_hbm, xall.at[r, 0], lsem.at[4]),
        pltpu.make_async_copy(tbasis_hbm, xall.at[r, 1], lsem.at[5]),
    ]
    blocks = [
        pltpu.make_async_copy(
            modes_hbm.at[:, pl.ds(b * TILE, TILE)], cin.at[b], bsem.at[b]
        )
        for b in range(8)
    ]
    chunks = [
        pltpu.make_async_copy(
            mass_hbm.at[pl.ds(i * CHUNK, CHUNK)], raw.at[pl.ds(i * CHUNK, CHUNK)], msem.at[i]
        )
        for i in range(CHUNKS)
    ]
    locals_[4].start()
    locals_[5].start()
    for b in range(8):
        blocks[b].start()
    chunks[0].start()
    chunks[1].start()
    locals_[2].start()
    locals_[3].start()
    for i in range(2, CHUNKS):
        chunks[i].start()
    locals_[1].start()

    barrier = pltpu.get_barrier_semaphore()

    @pl.loop(1, ROWS)
    def _(d):
        pl.semaphore_signal(
            barrier, inc=1, device_id=(lax.rem(r + d, ROWS), c), device_id_type=MESH
        )

    @pl.loop(1, COLS)
    def _(d):
        pl.semaphore_signal(
            barrier, inc=1, device_id=(r, lax.rem(c + d, COLS)), device_id_type=MESH
        )

    for b in range(16):
        maskrow[:, b * TILE : (b + 1) * TILE] = jnp.broadcast_to(
            mask_ref[:, b : b + 1].astype(F32), (16, TILE)
        )

    def apply_mask(i):
        chunks[i].wait()
        for half in range(CHUNK // TILE):
            rows = i * CHUNK + half * TILE
            a = i * (CHUNK // TILE) + half
            m = jnp.broadcast_to(maskrow[a : a + 1, :], (16, N)).astype(BF16)
            for q in range(TILE // 16):
                masked[i % 2, half * TILE + q * 16 : half * TILE + (q + 1) * 16, :] = (
                    raw[rows + q * 16 : rows + (q + 1) * 16, :] * m
                )

    for b in range(8):
        blocks[b].wait()
    for k in range(2):
        for i in range(4):
            at = 0
            for a in range(1, 4):
                at = at + a * is_block(map_ref[k, a], i)
            to = k * SEP + i * TILE
            cp[:, to : to + TILE] = cin[k * 4 + lax.rem(at, 4)]
    apply_mask(0)

    pl.semaphore_wait(barrier, ROWS - 1 + COLS - 1)
    locals_[4].wait()
    locals_[5].wait()

    def row_copy(d, src, dst, send, recv):
        return pltpu.make_async_remote_copy(
            src_ref=src,
            dst_ref=dst,
            send_sem=send.at[d],
            recv_sem=recv.at[d],
            device_id=(lax.rem(r + d, ROWS), c),
            device_id_type=MESH,
        )

    def col_copy(d, src, dst, send, recv):
        return pltpu.make_async_remote_copy(
            src_ref=src,
            dst_ref=dst,
            send_sem=send.at[d],
            recv_sem=recv.at[d],
            device_id=(r, lax.rem(c + d, COLS)),
            device_id_type=MESH,
        )

    def each_row(fn):
        @pl.loop(1, ROWS)
        def _(d):
            fn(d)

    def each_col(fn):
        @pl.loop(1, COLS)
        def _(d):
            fn(d)

    def src_row(d):
        return lax.rem(r + ROWS - d, ROWS)

    def src_col(d):
        return lax.rem(c + COLS - d, COLS)

    x_copy = lambda d: row_copy(d, xall.at[r], xall.at[r], x_send, x_recv)
    x_wait = lambda d: row_copy(d, xall.at[r], xall.at[src_row(d)], x_send, x_recv)
    each_row(lambda d: x_copy(d).start())

    for i in range(CHUNKS):
        if i + 1 < CHUNKS:
            apply_mask(i + 1)
        loaded[i * CHUNK : (i + 1) * CHUNK, :] = dot_nn(masked[i % 2], cp[...]).astype(BF16)

    each_row(lambda d: x_wait(d).wait_recv())

    part[0] = dot_tn(cp[:, 0:SEP], loaded[:, 0:SEP]).reshape(4, 4, 32, SEP)
    part[1] = dot_tn(cp[:, SEP:], loaded[:, SEP:]).reshape(4, 4, 32, SEP)
    locals_[2].wait()
    locals_[3].wait()
    part[0, z, x] = part[0, z, x] + gmass[...]
    own_rows = lax.div(lax.broadcasted_iota(jnp.int32, (32, SEP), 0), 4) == c
    own_top = jnp.concatenate([tmass[...]] * 8, axis=0)
    part[1, z, x] = part[1, z, x] + jnp.where(own_rows, own_top, 0.0)

    def ring(phase, arr):
        along_z = (arr == 0) == (phase == 1)
        me = z if along_z else x

        def device(step):
            to = lax.rem(me + step + 4, 4)
            return (to * 4 + x, c) if along_z else (z * 4 + to, c)

        return me, device

    def source(phase, arr, dest, half):
        if phase == 1:
            if arr == 0:
                return part.at[0, dest, pl.ds(half * 2, 2)]
            return part.at[1, pl.ds(half * 2, 2), dest]
        return s1.at[arr, dest, pl.ds(half * 16, 16)]

    boxes = {1: (opp1, own1, acc1), 2: (opp2, own2, acc2)}

    def ring_copy(phase, arr, kind, way, src):
        _, device = ring(phase, arr)
        slot = ((phase - 1) * 2 + arr) * 6 + kind * 2 + way
        return pltpu.make_async_remote_copy(
            src_ref=src,
            dst_ref=boxes[phase][kind].at[arr, way],
            send_sem=r_send.at[slot],
            recv_sem=r_recv.at[slot],
            device_id=device(1 - 2 * way),
            device_id_type=MESH,
        )

    def opp_copy(phase, arr, way):
        me, _ = ring(phase, arr)
        return ring_copy(phase, arr, 0, way, source(phase, arr, lax.rem(me + 2, 4), way))

    def own_copy(phase, arr, way):
        me, _ = ring(phase, arr)
        dest = lax.rem(me + 1 - 2 * way + 4, 4)
        return ring_copy(phase, arr, 1, way, source(phase, arr, dest, 1 - way))

    def acc_copy(phase, arr, way):
        return ring_copy(phase, arr, 2, way, boxes[phase][0].at[arr, way])

    def ring_open(phase, copies):
        for copy in copies:
            for arr in range(2):
                for way in range(2):
                    copy(phase, arr, way).start()

    def ring_pass(phase):
        for arr in range(2):
            me, _ = ring(phase, arr)
            for way in range(2):
                opp_copy(phase, arr, way).wait_recv()
                dest = lax.rem(me + 1 - 2 * way + 4, 4)
                box = boxes[phase][0].at[arr, way]
                box[...] = box[...] + source(phase, arr, dest, way)[...]
                acc_copy(phase, arr, way).start()

    def ring_close(phase, arr):
        me, _ = ring(phase, arr)
        halves = []
        for half in range(2):
            acc_copy(phase, arr, half).wait_recv()
            own_copy(phase, arr, 1 - half).wait_recv()
            halves.append(
                source(phase, arr, me, half)[...]
                + boxes[phase][2][arr, half]
                + boxes[phase][1][arr, 1 - half]
            )
        return halves

    def basis(m):
        return xall[:, m].reshape(SEP, 128)

    for m in (1, 0):
        x_high, x_low = split_two(basis(m))
        x_both = jnp.concatenate([x_high, x_low], axis=1)
        p_high, p_low = split_two(part[m].reshape(SEP, SEP))
        applied = dot_nn(p_high, x_both)
        applied = applied[:, 0:128] + applied[:, 128:256] + dot_nn(p_low, x_high)
        a_high, a_low = split_two(applied)
        term = dot_tn(x_both, a_high)
        gram[m] = term[0:128] + term[128:256] + dot_tn(x_high, a_low)
        if m == 1:
            for q in range(COLS):
                t_row[q] = gram[1, q * 16 : (q + 1) * 16, :]
            each_col(
                lambda d: col_copy(
                    d, t_row.at[lax.rem(c + d, COLS)], t_in.at[c], ta_send, ta_recv
                ).start()
            )
    for q in range(ROWS):
        g_sum[q] = gram[0, q * 8 : (q + 1) * 8, :]
    each_row(
        lambda d: row_copy(
            d, g_sum.at[lax.rem(r + d, ROWS)], g_in.at[r], g1_send, g1_recv
        ).start()
    )
    t_in[c] = t_row[c]
    g_in[r] = g_sum[r]

    ring_open(1, (opp_copy,))

    locals_[1].wait()
    projected = dot_tn(fixed[...], loaded[...])
    seen = [
        dot_nn(projected[:, m * SEP : (m + 1) * SEP], basis(m), precision=HIGHEST)
        for m in range(2)
    ]
    for m in range(2):
        seen_ref[m] = seen[m]

    each_col(
        lambda d: col_copy(d, t_row.at[0], t_in.at[src_col(d)], ta_send, ta_recv).wait_recv()
    )
    total = t_in[0]
    for q in range(1, COLS):
        total = total + t_in[q]
    t_sum[r] = total
    each_row(lambda d: row_copy(d, t_sum.at[r], t_sum.at[r], tb_send, tb_recv).start())

    each_row(
        lambda d: row_copy(d, g_sum.at[0], g_in.at[src_row(d)], g1_send, g1_recv).wait_recv()
    )
    total = g_in[0]
    for q in range(1, ROWS):
        total = total + g_in[q]
    g_all[r] = total
    each_row(lambda d: row_copy(d, g_all.at[r], g_all.at[r], g2_send, g2_recv).start())

    ring_open(1, (own_copy,))
    ring_pass(1)

    each_row(
        lambda d: row_copy(d, t_sum.at[r], t_sum.at[src_row(d)], tb_send, tb_recv).wait_recv()
    )
    total = t_sum[0]
    for q in range(1, ROWS):
        total = total + t_sum[q]
    t_all[c] = total
    each_col(lambda d: col_copy(d, t_all.at[c], t_all.at[c], tc_send, tc_recv).start())

    each_row(
        lambda d: row_copy(d, g_all.at[r], g_all.at[src_row(d)], g2_send, g2_recv).wait_recv()
    )
    each_col(
        lambda d: col_copy(d, t_all.at[c], t_all.at[src_col(d)], tc_send, tc_recv).wait_recv()
    )
    eye = (
        lax.broadcasted_iota(jnp.int32, (128, 128), 0)
        == lax.broadcasted_iota(jnp.int32, (128, 128), 1)
    ).astype(F32)
    for m, whole in enumerate((g_all[...], t_all[...])):
        whole = whole.reshape(128, 128)
        ch[m, :, 0:128] = 0.5 * (whole + whole.T)
        ch[m, :, 128:256] = eye

    def panels(lo, hi):
        for p in range(lo, hi):
            factor_panel(ch, w_ref, p)

    panels(0, 5)
    for arr in (1, 0):
        halves = ring_close(1, arr)
        s1[arr, 0:2] = halves[0]
        s1[arr, 2:4] = halves[1]
    ring_open(2, (opp_copy, own_copy))
    panels(5, 11)
    ring_pass(2)
    panels(11, 16)
    halves = ring_close(2, 1)
    for half in range(2):
        for q in range(4):
            tcol[half * 4 + q] = halves[half][q * 4 : (q + 1) * 4, :]
    each_col(
        lambda d: col_copy(
            d, tcol.at[lax.rem(c + d, COLS)], tcol_in.at[c], k_send, k_recv
        ).start()
    )
    tcol_in[c] = tcol[c]
    halves = ring_close(2, 0)
    for half in range(2):
        gout_ref[half * 16 : (half + 1) * 16, :] = SEP * halves[half]
    own_ref[...] = xall[r]

    each_col(
        lambda d: col_copy(d, tcol.at[0], tcol_in.at[src_col(d)], k_send, k_recv).wait_recv()
    )
    total = tcol_in[0]
    for q in range(1, COLS):
        total = total + tcol_in[q]
    apex_ref[...] = SEP * total

    def sends_row(d):
        x_copy(d).wait_send()
        row_copy(d, g_sum.at[0], g_in.at[r], g1_send, g1_recv).wait_send()
        row_copy(d, g_all.at[r], g_all.at[r], g2_send, g2_recv).wait_send()
        row_copy(d, t_sum.at[r], t_sum.at[r], tb_send, tb_recv).wait_send()

    def sends_col(d):
        col_copy(d, t_row.at[0], t_in.at[c], ta_send, ta_recv).wait_send()
        col_copy(d, t_all.at[c], t_all.at[c], tc_send, tc_recv).wait_send()
        col_copy(d, tcol.at[0], tcol_in.at[c], k_send, k_recv).wait_send()

    each_row(sends_row)
    each_col(sends_col)
    for phase in (1, 2):
        for copy in (opp_copy, own_copy, acc_copy):
            for arr in range(2):
                for way in range(2):
                    copy(phase, arr, way).wait_send()


def finish(seen, inverse, own, gmatrix, tmatrix, coup, gmodes, tmodes, gout, apex):
    gout[...] = gmatrix[...]
    apex[...] = tmatrix[...]
    for m, modes in enumerate((gmodes, tmodes)):
        coup[:, m, :] = dot_nt(seen[m], inverse[m], precision=HIGHEST)
        modes[...] = dot_nt(own[m], inverse[m], precision=HIGHEST)


def body(
    leaf_mass,
    tile_mask,
    constraint_modes,
    leaf_fixed_modes,
    block_map,
    group_mass,
    top_mass,
    group_basis,
    top_basis,
):
    hbm = pl.BlockSpec(memory_space=pl.ANY)
    vmem = pl.BlockSpec(memory_space=pltpu.VMEM)
    smem = pl.BlockSpec(memory_space=pltpu.SMEM)
    dma = pltpu.SemaphoreType.DMA
    half1 = (2, 2, 2, 32, SEP)
    half2 = (2, 2, 16, SEP)
    scratch = [
        pltpu.VMEM((N, N), BF16),
        pltpu.VMEM((2, CHUNK, N), BF16),
        pltpu.VMEM((8, N, TILE), BF16),
        pltpu.VMEM((N, 2 * SEP), BF16),
        pltpu.VMEM((N, 2 * SEP), BF16),
        pltpu.VMEM((N, 128), BF16),
        pltpu.VMEM((16, N), F32),
        pltpu.VMEM((32, SEP), F32),
        pltpu.VMEM((4, SEP), F32),
        pltpu.VMEM((ROWS, 2, 32, 128), F32),
        pltpu.VMEM((2, 4, 4, 32, SEP), F32),
        pltpu.VMEM((2, 128, 128), F32),
        pltpu.VMEM((ROWS, 8, 128), F32),
        pltpu.VMEM((ROWS, 8, 128), F32),
        pltpu.VMEM((ROWS, 8, 128), F32),
        pltpu.VMEM((COLS, 16, 128), F32),
        pltpu.VMEM((ROWS, 16, 128), F32),
        pltpu.VMEM((COLS, 16, 128), F32),
        pltpu.VMEM((COLS, 16, 128), F32),
        pltpu.VMEM((COLS, 16, 128), F32),
        pltpu.VMEM(half1, F32),
        pltpu.VMEM(half1, F32),
        pltpu.VMEM(half1, F32),
        pltpu.VMEM((2, 4, 32, SEP), F32),
        pltpu.VMEM(half2, F32),
        pltpu.VMEM(half2, F32),
        pltpu.VMEM(half2, F32),
        pltpu.VMEM((COLS, 4, SEP), F32),
        pltpu.VMEM((COLS, 4, SEP), F32),
        pltpu.VMEM((2, 128, 256), F32),
        dma((6,)),
        dma((8,)),
        dma((CHUNKS,)),
        dma((ROWS,)),
        dma((ROWS,)),
        dma((ROWS,)),
        dma((ROWS,)),
        dma((ROWS,)),
        dma((ROWS,)),
        dma((COLS,)),
        dma((COLS,)),
        dma((ROWS,)),
        dma((ROWS,)),
        dma((COLS,)),
        dma((COLS,)),
        dma((24,)),
        dma((24,)),
        dma((COLS,)),
        dma((COLS,)),
    ]
    seen, inverse, own, gout, apex = pl.pallas_call(
        kernel,
        out_shape=(
            jax.ShapeDtypeStruct((2, 128, 128), F32),
            jax.ShapeDtypeStruct((2, 128, 128), F32),
            jax.ShapeDtypeStruct((2, 32, 128), F32),
            jax.ShapeDtypeStruct((32, SEP), F32),
            jax.ShapeDtypeStruct((4, SEP), F32),
        ),
        in_specs=[hbm, vmem, hbm, hbm, smem, hbm, hbm, hbm, hbm],
        out_specs=(vmem, vmem, vmem, vmem, vmem),
        scratch_shapes=scratch,
        compiler_params=pltpu.CompilerParams(
            collective_id=0, has_side_effects=True, vmem_limit_bytes=60 << 20
        ),
        name="assemble",
    )(
        leaf_mass[0],
        tile_mask[0],
        constraint_modes[0],
        leaf_fixed_modes[0],
        block_map[0],
        group_mass[0],
        top_mass,
        group_basis[0],
        top_basis,
    )
    coupling, gmodes, tmodes, gout, apex = pl.pallas_call(
        finish,
        out_shape=(
            jax.ShapeDtypeStruct((128, 2, 128), F32),
            jax.ShapeDtypeStruct((32, 128), F32),
            jax.ShapeDtypeStruct((32, 128), F32),
            jax.ShapeDtypeStruct((32, SEP), F32),
            jax.ShapeDtypeStruct((4, SEP), F32),
        ),
        in_specs=[vmem] * 5,
        out_specs=(vmem,) * 5,
        name="finish",
    )(seen, inverse, own, gout, apex)
    return (coupling[None], gmodes[None], tmodes, gout[None], apex)


def solution(mesh):
    in_specs = (
        P(("row", "col"), None, None),
        P(("row", "col"), None, None),
        P(("row", "col"), None, None),
        P(("row", "col"), None, None),
        P(("row", "col"), None, None),
        P("col", "row", None),
        P(("row", "col"), None),
        P("col", "row", None),
        P("row", None),
    )
    out_specs = (
        P(("row", "col"), None, None, None),
        P("col", "row", None),
        P("row", None),
        P("col", "row", None),
        P(("row", "col"), None),
    )
    return jax.shard_map(body, mesh=mesh, in_specs=in_specs, out_specs=out_specs, check_vma=False)
```

```python
import jax
import jax.numpy as jnp
from jax import lax
from jax.experimental import pallas as pl
from jax.experimental.pallas import tpu as pltpu
from jax.sharding import PartitionSpec as P

TILE = 128
SEP = 512
ROWS = 16
COLS = 8
PLANE = 32
N = 2048
CHUNK = 1024
CHUNKS = N // CHUNK
F32 = jnp.float32
BF16 = jnp.bfloat16
MESH = pl.DeviceIdType.MESH
HIGHEST = lax.Precision.HIGHEST


def dot_tn(a, b, **kw):
    return lax.dot_general(a, b, (((0,), (0,)), ((), ())), preferred_element_type=F32, **kw)


def dot_nt(a, b, **kw):
    return lax.dot_general(a, b, (((1,), (1,)), ((), ())), preferred_element_type=F32, **kw)


def dot_nn(a, b, **kw):
    return jnp.dot(a, b, preferred_element_type=F32, **kw)


def split_three(u):
    a = u.astype(BF16).astype(F32)
    rest = u - a
    b = rest.astype(BF16).astype(F32)
    c = rest - b
    return a, b, c


def is_block(value, i):
    top, below = 1, 1
    for j in range(4):
        if j != i:
            top = top * (value - j)
            below = below * (i - j)
    return lax.div(top * (1 if below > 0 else -1), abs(below))


def factor_panel(ch, w, p):
    k = p * 8
    sub = lax.broadcasted_iota(jnp.int32, (8, 128), 0)
    for m in range(2):
        pa = ch[m, k : k + 8, 0:128]
        pw = ch[m, k : k + 8, 128:256]
        c = [jnp.broadcast_to(pa[:, k + j : k + j + 1], (8, 128)) for j in range(8)]
        scale = jnp.zeros((8, 128), F32)
        for j in range(8):
            pivot = jnp.broadcast_to(c[j][j : j + 1, :], (8, 128))
            root = lax.rsqrt(pivot)
            scale = jnp.where(sub == j, root, scale)
            if j < 7:
                f = jnp.where(sub > j, c[j] * (root * root), 0.0)
                pa = pa - f * jnp.broadcast_to(pa[j : j + 1, :], (8, 128))
                pw = pw - f * jnp.broadcast_to(pw[j : j + 1, :], (8, 128))
                for q in range(j + 1, 8):
                    c[q] = c[q] - f * jnp.broadcast_to(c[q][j : j + 1, :], (8, 128))
        ua = pa * scale
        uw = pw * scale
        w[m, k : k + 8, :] = uw
        if p == 15:
            continue
        a1, a2, a3 = split_three(ua)
        w1, w2, w3 = split_three(uw)
        left = jnp.concatenate([a1, a1, a2, a2, a1, a3], axis=0).astype(BF16)
        right = jnp.concatenate(
            [
                jnp.concatenate([a1, a2, a1, a2, a3, a1], axis=0),
                jnp.concatenate([w1, w2, w1, w2, w3, w1], axis=0),
            ],
            axis=1,
        ).astype(BF16)
        ch[m, k + 8 :] = ch[m, k + 8 :] - dot_tn(left, right)[k + 8 :]


def split_two(v):
    high = v.astype(BF16)
    return high, (v - high.astype(F32)).astype(BF16)


def kernel(
    mass_hbm,
    mask_ref,
    modes_hbm,
    fixed_hbm,
    map_ref,
    gmass_hbm,
    tmass_hbm,
    gbasis_hbm,
    tbasis_hbm,
    seen_ref,
    w_ref,
    own_ref,
    gout_ref,
    apex_ref,
    raw,
    masked,
    cin,
    cp,
    loaded,
    fixed,
    maskrow,
    gmass,
    tmass,
    xall,
    pg,
    pt,
    swapped,
    gram,
    g_in,
    g_sum,
    g_all,
    t_in,
    t_sum,
    t_row,
    t_fin,
    t_all,
    opp1g,
    own1g,
    acc1g,
    opp1t,
    own1t,
    acc1t,
    sg,
    opp2g,
    own2g,
    acc2g,
    tcol,
    tcol_in,
    ch,
    lsem,
    bsem,
    msem,
    x_send,
    x_recv,
    g1_send,
    g1_recv,
    g2_send,
    g2_recv,
    ta_send,
    ta_recv,
    tb_send,
    tb_recv,
    tc_send,
    tc_recv,
    r_send,
    r_recv,
    k_send,
    k_recv,
    w_sem,
):
    r = lax.axis_index("row")
    c = lax.axis_index("col")
    z = lax.div(r, 4)
    x = lax.rem(r, 4)
    slot = z * COLS + c
    core = lax.rem(c, 2)

    locals_ = [
        None,
        pltpu.make_async_copy(fixed_hbm, fixed, lsem.at[1]),
        pltpu.make_async_copy(gmass_hbm, gmass, lsem.at[2]),
        pltpu.make_async_copy(tmass_hbm, tmass, lsem.at[3]),
        pltpu.make_async_copy(gbasis_hbm, xall.at[r, 0], lsem.at[4]),
        pltpu.make_async_copy(tbasis_hbm, xall.at[r, 1], lsem.at[5]),
    ]
    blocks = [
        pltpu.make_async_copy(
            modes_hbm.at[:, pl.ds(b * TILE, TILE)], cin.at[b], bsem.at[b]
        )
        for b in range(8)
    ]
    chunks = [
        pltpu.make_async_copy(
            mass_hbm.at[pl.ds(i * CHUNK, CHUNK)], raw.at[pl.ds(i * CHUNK, CHUNK)], msem.at[i]
        )
        for i in range(CHUNKS)
    ]
    locals_[4].start()
    locals_[5].start()
    for b in range(8):
        blocks[b].start()
    chunks[0].start()
    chunks[1].start()
    locals_[2].start()
    locals_[3].start()
    for i in range(2, CHUNKS):
        chunks[i].start()
    locals_[1].start()

    barrier = pltpu.get_barrier_semaphore()

    @pl.loop(1, ROWS)
    def _(d):
        pl.semaphore_signal(
            barrier, inc=1, device_id=(lax.rem(r + d, ROWS), c), device_id_type=MESH
        )

    @pl.loop(0, 4)
    def _(up):
        @pl.loop(1, COLS)
        def _(d):
            pl.semaphore_signal(
                barrier,
                inc=1,
                device_id=(lax.rem(z + up, 4) * 4 + x, lax.rem(c + d, COLS)),
                device_id_type=MESH,
            )

    for b in range(16):
        maskrow[:, b * TILE : (b + 1) * TILE] = jnp.broadcast_to(
            mask_ref[:, b : b + 1].astype(F32), (16, TILE)
        )

    def apply_mask(i):
        chunks[i].wait()
        for half in range(CHUNK // TILE):
            rows = i * CHUNK + half * TILE
            a = i * (CHUNK // TILE) + half
            m = jnp.broadcast_to(maskrow[a : a + 1, :], (16, N)).astype(BF16)
            for q in range(TILE // 16):
                masked[i, half * TILE + q * 16 : half * TILE + (q + 1) * 16, :] = (
                    raw[rows + q * 16 : rows + (q + 1) * 16, :] * m
                )

    for b in range(8):
        blocks[b].wait()
    for k in range(2):
        for i in range(4):
            at = 0
            for a in range(1, 4):
                at = at + a * is_block(map_ref[k, a], i)
            to = k * SEP + i * TILE
            cp[:, to : to + TILE] = cin[k * 4 + lax.rem(at, 4)]
    apply_mask(0)

    def row_copy(d, src, dst, send, recv):
        return pltpu.make_async_remote_copy(
            src_ref=src,
            dst_ref=dst,
            send_sem=send.at[d],
            recv_sem=recv.at[d],
            device_id=(lax.rem(r + d, ROWS), c),
            device_id_type=MESH,
        )

    def col_copy(d, src, dst, send, recv):
        return pltpu.make_async_remote_copy(
            src_ref=src,
            dst_ref=dst,
            send_sem=send.at[d],
            recv_sem=recv.at[d],
            device_id=(r, lax.rem(c + d, COLS)),
            device_id_type=MESH,
        )

    def each_row(fn):
        @pl.loop(1, ROWS)
        def _(d):
            fn(d)

    def each_col(fn):
        @pl.loop(1, COLS)
        def _(d):
            fn(d)

    def src_row(d):
        return lax.rem(r + ROWS - d, ROWS)

    def src_col(d):
        return lax.rem(c + COLS - d, COLS)

    def x_copy(d, m, at):
        return pltpu.make_async_remote_copy(
            src_ref=xall.at[r, m],
            dst_ref=xall.at[at, m],
            send_sem=x_send.at[m, d],
            recv_sem=x_recv.at[m, d],
            device_id=(lax.rem(r + d, ROWS), c),
            device_id_type=MESH,
        )

    def k_copy(d, at):
        s = lax.rem(slot + d, PLANE)
        return pltpu.make_async_remote_copy(
            src_ref=tcol.at[s],
            dst_ref=tcol_in.at[at],
            send_sem=k_send.at[d],
            recv_sem=k_recv.at[d],
            device_id=(lax.div(s, COLS) * 4 + x, lax.rem(s, COLS)),
            device_id_type=MESH,
        )
    def load_columns(i, m):
        cols = slice(m * SEP, (m + 1) * SEP)
        loaded[i * CHUNK : (i + 1) * CHUNK, cols] = dot_nn(masked[i], cp[:, cols]).astype(BF16)

    def basis(m):
        return xall[:, m].reshape(SEP, 128)

    def gram_of(matrix, m):
        x_high, x_low = split_two(basis(m))
        x_both = jnp.concatenate([x_high, x_low], axis=1)
        p_high, p_low = split_two(matrix)
        applied = dot_nn(p_high, x_both)
        applied = applied[:, 0:128] + applied[:, 128:256] + dot_nn(p_low, x_high)
        a_high, a_low = split_two(applied)
        term = dot_tn(x_both, a_high)
        gram[m] = term[0:128] + term[128:256] + dot_tn(x_high, a_low)

    def ring(phase, arr):
        along_z = (arr == 0) == (phase == 1)
        me = z if along_z else x

        def device(step):
            to = lax.rem(me + step + 4, 4)
            return (to * 4 + x, c) if along_z else (z * 4 + to, c)

        return me, device

    def source(phase, arr, dest, half):
        if phase == 1:
            if arr == 0:
                return pg.at[0, dest, pl.ds(half * 2, 2)]
            if arr == 2:
                return pg.at[1, pl.ds(half * 2, 2), dest]
            return pt.at[core, pl.ds(half * 2, 2), dest]
        return sg.at[arr // 2, dest, pl.ds(half * 16, 16)]

    boxes = {
        (1, 0): (opp1g, own1g, acc1g),
        (1, 1): (opp1t, own1t, acc1t),
        (2, 0): (opp2g, own2g, acc2g),
    }

    def box_of(phase, arr, kind, way):
        if arr == 1:
            return boxes[phase, 1][kind].at[way]
        return boxes[phase, 0][kind].at[arr // 2, way]

    def ring_copy(phase, arr, kind, way, src):
        _, device = ring(phase, arr)
        sem = ((phase - 1) * 3 + arr) * 6 + kind * 2 + way
        return pltpu.make_async_remote_copy(
            src_ref=src,
            dst_ref=box_of(phase, arr, kind, way),
            send_sem=r_send.at[sem],
            recv_sem=r_recv.at[sem],
            device_id=device(1 - 2 * way),
            device_id_type=MESH,
        )

    def opp_copy(phase, arr, way):
        me, _ = ring(phase, arr)
        return ring_copy(phase, arr, 0, way, source(phase, arr, lax.rem(me + 2, 4), way))

    def own_copy(phase, arr, way):
        me, _ = ring(phase, arr)
        dest = lax.rem(me + 1 - 2 * way + 4, 4)
        return ring_copy(phase, arr, 1, way, source(phase, arr, dest, 1 - way))

    def acc_copy(phase, arr, way):
        return ring_copy(phase, arr, 2, way, box_of(phase, arr, 0, way))

    def ring_start(phase, arrs, copy):
        for arr in arrs:
            for way in range(2):
                copy(phase, arr, way).start()

    def ring_pass(phase, arrs):
        for arr in arrs:
            me, _ = ring(phase, arr)
            for way in range(2):
                opp_copy(phase, arr, way).wait_recv()
                dest = lax.rem(me + 1 - 2 * way + 4, 4)
                box = box_of(phase, arr, 0, way)
                box[...] = box[...] + source(phase, arr, dest, way)[...]
                acc_copy(phase, arr, way).start()

    def ring_close(phase, arr):
        me, _ = ring(phase, arr)
        halves = []
        for half in range(2):
            acc_copy(phase, arr, half).wait_recv()
            own_copy(phase, arr, 1 - half).wait_recv()
            halves.append(
                source(phase, arr, me, half)[...]
                + box_of(phase, arr, 2, half)[...]
                + box_of(phase, arr, 1, 1 - half)[...]
            )
        return halves

    load_columns(0, 1)
    pl.semaphore_wait(barrier, ROWS - 1 + 4 * (COLS - 1))
    locals_[5].wait()
    each_row(lambda d: x_copy(d, 1, r).start())
    locals_[4].wait()
    each_row(lambda d: x_copy(d, 0, r).start())
    apply_mask(1)
    load_columns(1, 1)
    load_columns(0, 0)
    load_columns(1, 0)
    top = dot_tn(cp[:, SEP:], loaded[:, SEP:])
    for h in range(2):
        pt[h] = top[:, h * 256 : (h + 1) * 256].reshape(4, 4, 32, 256)
    locals_[3].wait()
    own_rows = lax.div(lax.broadcasted_iota(jnp.int32, (32, 256), 0), 4) == c
    own_top = jnp.concatenate([tmass[...]] * 8, axis=0)
    for h in range(2):
        pt[h, z, x] = pt[h, z, x] + jnp.where(own_rows, own_top[:, h * 256 : (h + 1) * 256], 0.0)
    swap = pltpu.make_async_remote_copy(
        src_ref=pt.at[1 - core],
        dst_ref=swapped,
        send_sem=w_sem.at[0],
        recv_sem=w_sem.at[1],
        device_id=(r, c + 1 - 2 * core),
        device_id_type=MESH,
    )
    swap.start()
    each_row(lambda d: x_copy(d, 1, src_row(d)).wait_recv())
    gram_of(
        jnp.concatenate([pt[0].reshape(SEP, 256), pt[1].reshape(SEP, 256)], axis=1), 1
    )
    for q in range(COLS):
        t_row[q] = gram[1, q * 16 : (q + 1) * 16, :]
    each_col(
        lambda d: col_copy(
            d, t_row.at[lax.rem(c + d, COLS)], t_in.at[c], ta_send, ta_recv
        ).start()
    )
    t_in[c] = t_row[c]
    swap.wait_recv()
    pt[core] = pt[core] + swapped[...]
    ring_start(1, (1,), opp_copy)

    group = dot_tn(cp[:, 0:SEP], loaded[:, 0:SEP])
    for h in range(2):
        pg[h] = group[:, h * 256 : (h + 1) * 256].reshape(4, 4, 32, 256)
    locals_[2].wait()
    for h in range(2):
        pg[h, z, x] = pg[h, z, x] + gmass[:, h * 256 : (h + 1) * 256]
    each_row(lambda d: x_copy(d, 0, src_row(d)).wait_recv())
    gram_of(
        jnp.concatenate([pg[0].reshape(SEP, 256), pg[1].reshape(SEP, 256)], axis=1), 0
    )
    for q in range(ROWS):
        g_sum[q] = gram[0, q * 8 : (q + 1) * 8, :]
    each_row(
        lambda d: row_copy(
            d, g_sum.at[lax.rem(r + d, ROWS)], g_in.at[r], g1_send, g1_recv
        ).start()
    )
    g_in[r] = g_sum[r]
    ring_start(1, (0, 2), opp_copy)

    locals_[1].wait()
    projected = dot_tn(fixed[...], loaded[...])
    for m in range(2):
        seen_ref[m] = dot_nn(
            projected[:, m * SEP : (m + 1) * SEP], basis(m), precision=HIGHEST
        )
    own_ref[...] = xall[r]

    each_col(
        lambda d: col_copy(d, t_row.at[0], t_in.at[src_col(d)], ta_send, ta_recv).wait_recv()
    )
    total = t_in[0]
    for q in range(1, COLS):
        total = total + t_in[q]
    t_sum[r] = total
    each_row(lambda d: row_copy(d, t_sum.at[r], t_sum.at[r], tb_send, tb_recv).start())
    ring_start(1, (1,), own_copy)

    each_row(
        lambda d: row_copy(d, g_sum.at[0], g_in.at[src_row(d)], g1_send, g1_recv).wait_recv()
    )
    total = g_in[0]
    for q in range(1, ROWS):
        total = total + g_in[q]
    g_all[r] = total
    each_row(lambda d: row_copy(d, g_all.at[r], g_all.at[r], g2_send, g2_recv).start())
    ring_start(1, (0, 2), own_copy)
    ring_pass(1, (1, 0, 2))

    each_row(
        lambda d: row_copy(d, t_sum.at[r], t_sum.at[src_row(d)], tb_send, tb_recv).wait_recv()
    )
    total = t_sum[0]
    for q in range(1, ROWS):
        total = total + t_sum[q]
    t_all[c] = total
    each_col(lambda d: col_copy(d, t_all.at[c], t_all.at[c], tc_send, tc_recv).start())

    eye = (
        lax.broadcasted_iota(jnp.int32, (128, 128), 0)
        == lax.broadcasted_iota(jnp.int32, (128, 128), 1)
    ).astype(F32)

    def start_factor(m, whole):
        whole = whole.reshape(128, 128)
        ch[m, :, 0:128] = 0.5 * (whole + whole.T)
        ch[m, :, 128:256] = eye

    def panels(lo, hi):
        for p in range(lo, hi):
            factor_panel(ch, w_ref, p)

    for arr in (0, 2):
        halves = ring_close(1, arr)
        sg[arr // 2, 0:2] = halves[0]
        sg[arr // 2, 2:4] = halves[1]
    ring_start(2, (0, 2), opp_copy)
    ring_start(2, (0, 2), own_copy)

    each_row(
        lambda d: row_copy(d, g_all.at[r], g_all.at[src_row(d)], g2_send, g2_recv).wait_recv()
    )
    start_factor(0, g_all[...])
    each_col(
        lambda d: col_copy(d, t_all.at[c], t_all.at[src_col(d)], tc_send, tc_recv).wait_recv()
    )
    start_factor(1, t_all[...])

    halves = ring_close(1, 1)
    for half in range(2):
        for i in range(2):
            for q in range(COLS):
                tcol[(half * 2 + i) * COLS + q] = halves[half][i, q * 4 : (q + 1) * 4, :]

    @pl.loop(1, PLANE)
    def _(d):
        k_copy(d, slot).start()

    tcol_in[slot] = tcol[slot]
    panels(0, 8)
    ring_pass(2, (0, 2))
    panels(8, 16)
    for arr in (0, 2):
        halves = ring_close(2, arr)
        for half in range(2):
            gout_ref[half * 16 : (half + 1) * 16, arr * 128 : arr * 128 + 256] = SEP * halves[half]

    @pl.loop(1, PLANE)
    def _(d):
        k_copy(d, lax.rem(slot + PLANE - d, PLANE)).wait_recv()

    for h in range(2):
        total = tcol_in[h]
        for q in range(h + 2, PLANE, 2):
            total = total + tcol_in[q]
        apex_ref[:, h * 256 : (h + 1) * 256] = SEP * total

    def sends_row(d):
        x_copy(d, 0, r).wait_send()
        x_copy(d, 1, r).wait_send()
        row_copy(d, g_sum.at[0], g_in.at[r], g1_send, g1_recv).wait_send()
        row_copy(d, g_all.at[r], g_all.at[r], g2_send, g2_recv).wait_send()
        row_copy(d, t_sum.at[r], t_sum.at[r], tb_send, tb_recv).wait_send()

    def sends_col(d):
        col_copy(d, t_row.at[0], t_in.at[c], ta_send, ta_recv).wait_send()
        col_copy(d, t_all.at[c], t_all.at[c], tc_send, tc_recv).wait_send()

    swap.wait_send()
    each_row(sends_row)
    each_col(sends_col)

    @pl.loop(1, PLANE)
    def _(d):
        k_copy(d, slot).wait_send()

    for phase, arrs in ((1, (0, 1, 2)), (2, (0, 2))):
        for copy in (opp_copy, own_copy, acc_copy):
            for arr in arrs:
                for way in range(2):
                    copy(phase, arr, way).wait_send()


def finish(seen, inverse, own, gmatrix, tmatrix, coup, gmodes, tmodes, gout, apex):
    gout[...] = gmatrix[...]
    apex[...] = tmatrix[...]
    for m, modes in enumerate((gmodes, tmodes)):
        coup[:, m, :] = dot_nt(seen[m], inverse[m], precision=HIGHEST)
        modes[...] = dot_nt(own[m], inverse[m], precision=HIGHEST)


def body(
    leaf_mass,
    tile_mask,
    constraint_modes,
    leaf_fixed_modes,
    block_map,
    group_mass,
    top_mass,
    group_basis,
    top_basis,
):
    hbm = pl.BlockSpec(memory_space=pl.ANY)
    vmem = pl.BlockSpec(memory_space=pltpu.VMEM)
    smem = pl.BlockSpec(memory_space=pltpu.SMEM)
    dma = pltpu.SemaphoreType.DMA
    half1g = (2, 2, 2, 32, SEP // 2)
    half1t = (2, 2, 32, SEP // 2)
    half2g = (2, 2, 16, SEP // 2)
    scratch = [
        pltpu.VMEM((N, N), BF16),
        pltpu.VMEM((2, CHUNK, N), BF16),
        pltpu.VMEM((8, N, TILE), BF16),
        pltpu.VMEM((N, 2 * SEP), BF16),
        pltpu.VMEM((N, 2 * SEP), BF16),
        pltpu.VMEM((N, 128), BF16),
        pltpu.VMEM((16, N), F32),
        pltpu.VMEM((32, SEP), F32),
        pltpu.VMEM((4, SEP), F32),
        pltpu.VMEM((ROWS, 2, 32, 128), F32),
        pltpu.VMEM((2, 4, 4, 32, SEP // 2), F32),
        pltpu.VMEM((2, 4, 4, 32, SEP // 2), F32),
        pltpu.VMEM((4, 4, 32, SEP // 2), F32),
        pltpu.VMEM((2, 128, 128), F32),
        pltpu.VMEM((ROWS, 8, 128), F32),
        pltpu.VMEM((ROWS, 8, 128), F32),
        pltpu.VMEM((ROWS, 8, 128), F32),
        pltpu.VMEM((COLS, 16, 128), F32),
        pltpu.VMEM((ROWS, 16, 128), F32),
        pltpu.VMEM((COLS, 16, 128), F32),
        pltpu.VMEM((COLS, 16, 128), F32),
        pltpu.VMEM((COLS, 16, 128), F32),
        pltpu.VMEM(half1g, F32),
        pltpu.VMEM(half1g, F32),
        pltpu.VMEM(half1g, F32),
        pltpu.VMEM(half1t, F32),
        pltpu.VMEM(half1t, F32),
        pltpu.VMEM(half1t, F32),
        pltpu.VMEM((2, 4, 32, SEP // 2), F32),
        pltpu.VMEM(half2g, F32),
        pltpu.VMEM(half2g, F32),
        pltpu.VMEM(half2g, F32),
        pltpu.VMEM((PLANE, 4, SEP // 2), F32),
        pltpu.VMEM((PLANE, 4, SEP // 2), F32),
        pltpu.VMEM((2, 128, 256), F32),
        dma((6,)),
        dma((8,)),
        dma((CHUNKS,)),
        dma((2, ROWS)),
        dma((2, ROWS)),
        dma((ROWS,)),
        dma((ROWS,)),
        dma((ROWS,)),
        dma((ROWS,)),
        dma((COLS,)),
        dma((COLS,)),
        dma((ROWS,)),
        dma((ROWS,)),
        dma((COLS,)),
        dma((COLS,)),
        dma((36,)),
        dma((36,)),
        dma((PLANE,)),
        dma((PLANE,)),
        dma((2,)),
    ]
    seen, inverse, own, gout, apex = pl.pallas_call(
        kernel,
        out_shape=(
            jax.ShapeDtypeStruct((2, 128, 128), F32),
            jax.ShapeDtypeStruct((2, 128, 128), F32),
            jax.ShapeDtypeStruct((2, 32, 128), F32),
            jax.ShapeDtypeStruct((32, SEP), F32),
            jax.ShapeDtypeStruct((4, SEP), F32),
        ),
        in_specs=[hbm, vmem, hbm, hbm, smem, hbm, hbm, hbm, hbm],
        out_specs=(vmem, vmem, vmem, vmem, vmem),
        scratch_shapes=scratch,
        compiler_params=pltpu.CompilerParams(
            collective_id=0, has_side_effects=True, vmem_limit_bytes=60 << 20
        ),
        name="assemble",
    )(
        leaf_mass[0],
        tile_mask[0],
        constraint_modes[0],
        leaf_fixed_modes[0],
        block_map[0],
        group_mass[0],
        top_mass,
        group_basis[0],
        top_basis,
    )
    coupling, gmodes, tmodes, gout, apex = pl.pallas_call(
        finish,
        out_shape=(
            jax.ShapeDtypeStruct((128, 2, 128), F32),
            jax.ShapeDtypeStruct((32, 128), F32),
            jax.ShapeDtypeStruct((32, 128), F32),
            jax.ShapeDtypeStruct((32, SEP), F32),
            jax.ShapeDtypeStruct((4, SEP), F32),
        ),
        in_specs=[vmem] * 5,
        out_specs=(vmem,) * 5,
        name="finish",
    )(seen, inverse, own, gout, apex)
    return (coupling[None], gmodes[None], tmodes, gout[None], apex)


def solution(mesh):
    in_specs = (
        P(("row", "col"), None, None),
        P(("row", "col"), None, None),
        P(("row", "col"), None, None),
        P(("row", "col"), None, None),
        P(("row", "col"), None, None),
        P("col", "row", None),
        P(("row", "col"), None),
        P("col", "row", None),
        P("row", None),
    )
    out_specs = (
        P(("row", "col"), None, None, None),
        P("col", "row", None),
        P("row", None),
        P("col", "row", None),
        P(("row", "col"), None),
    )
    return jax.shard_map(body, mesh=mesh, in_specs=in_specs, out_specs=out_specs, check_vma=False)
```

```python
import jax
import jax.numpy as jnp
from jax import lax
from jax.experimental import pallas as pl
from jax.experimental.pallas import tpu as pltpu
from jax.sharding import PartitionSpec as P

TILE = 128
SEP = 512
ROWS = 16
COLS = 8
PLANE = 32
N = 2048
CHUNK = 1024
CHUNKS = N // CHUNK
F32 = jnp.float32
BF16 = jnp.bfloat16
MESH = pl.DeviceIdType.MESH
HIGHEST = lax.Precision.HIGHEST


def dot_tn(a, b, **kw):
    return lax.dot_general(a, b, (((0,), (0,)), ((), ())), preferred_element_type=F32, **kw)


def dot_nt(a, b, **kw):
    return lax.dot_general(a, b, (((1,), (1,)), ((), ())), preferred_element_type=F32, **kw)


def dot_nn(a, b, **kw):
    return jnp.dot(a, b, preferred_element_type=F32, **kw)


def split_three(u):
    a = u.astype(BF16).astype(F32)
    rest = u - a
    b = rest.astype(BF16).astype(F32)
    c = rest - b
    return a, b, c


def is_block(value, i):
    top, below = 1, 1
    for j in range(4):
        if j != i:
            top = top * (value - j)
            below = below * (i - j)
    return lax.div(top * (1 if below > 0 else -1), abs(below))


def factor_panel(ch, w, p):
    k = p * 8
    sub = lax.broadcasted_iota(jnp.int32, (8, 128), 0)
    for m in range(2):
        pa = ch[m, k : k + 8, 0:128]
        pw = ch[m, k : k + 8, 128:256]
        c = [jnp.broadcast_to(pa[:, k + j : k + j + 1], (8, 128)) for j in range(8)]
        scale = jnp.zeros((8, 128), F32)
        for j in range(8):
            pivot = jnp.broadcast_to(c[j][j : j + 1, :], (8, 128))
            root = lax.rsqrt(pivot)
            scale = jnp.where(sub == j, root, scale)
            if j < 7:
                f = jnp.where(sub > j, c[j] * (root * root), 0.0)
                pa = pa - f * jnp.broadcast_to(pa[j : j + 1, :], (8, 128))
                pw = pw - f * jnp.broadcast_to(pw[j : j + 1, :], (8, 128))
                for q in range(j + 1, 8):
                    c[q] = c[q] - f * jnp.broadcast_to(c[q][j : j + 1, :], (8, 128))
        ua = pa * scale
        uw = pw * scale
        w[m, k : k + 8, :] = uw
        if p == 15:
            continue
        a1, a2, a3 = split_three(ua)
        w1, w2, w3 = split_three(uw)
        left = jnp.concatenate([a1, a1, a2, a2, a1, a3], axis=0).astype(BF16)
        right = jnp.concatenate(
            [
                jnp.concatenate([a1, a2, a1, a2, a3, a1], axis=0),
                jnp.concatenate([w1, w2, w1, w2, w3, w1], axis=0),
            ],
            axis=1,
        ).astype(BF16)
        ch[m, k + 8 :] = ch[m, k + 8 :] - dot_tn(left, right)[k + 8 :]


def split_two(v):
    high = v.astype(BF16)
    return high, (v - high.astype(F32)).astype(BF16)


def kernel(
    mass_hbm,
    mask_ref,
    modes_hbm,
    fixed_hbm,
    map_ref,
    gmass_hbm,
    tmass_hbm,
    gbasis_hbm,
    tbasis_hbm,
    seen_ref,
    w_ref,
    own_ref,
    gout_ref,
    apex_ref,
    raw,
    masked,
    cin,
    cp,
    loaded,
    fixed,
    maskrow,
    gmass,
    tmass,
    xall,
    pg,
    pt,
    swapped,
    gram,
    g_in,
    g_sum,
    g_all,
    t_in,
    t_sum,
    t_row,
    t_fin,
    t_all,
    opp1g,
    own1g,
    acc1g,
    opp1t,
    own1t,
    acc1t,
    sg,
    opp2g,
    own2g,
    acc2g,
    tcol,
    tcol_in,
    ch,
    lsem,
    bsem,
    msem,
    x_send,
    x_recv,
    g1_send,
    g1_recv,
    g2_send,
    g2_recv,
    ta_send,
    ta_recv,
    tb_send,
    tb_recv,
    tc_send,
    tc_recv,
    r_send,
    r_recv,
    k_send,
    k_recv,
    w_sem,
):
    r = lax.axis_index("row")
    c = lax.axis_index("col")
    z = lax.div(r, 4)
    x = lax.rem(r, 4)
    slot = z * COLS + c
    core = lax.rem(c, 2)

    locals_ = [
        None,
        pltpu.make_async_copy(fixed_hbm, fixed, lsem.at[1]),
        pltpu.make_async_copy(gmass_hbm, gmass, lsem.at[2]),
        pltpu.make_async_copy(tmass_hbm, tmass, lsem.at[3]),
        pltpu.make_async_copy(gbasis_hbm, xall.at[r, 0], lsem.at[4]),
        pltpu.make_async_copy(tbasis_hbm, xall.at[r, 1], lsem.at[5]),
    ]
    blocks = [
        pltpu.make_async_copy(
            modes_hbm.at[:, pl.ds(b * TILE, TILE)], cin.at[b], bsem.at[b]
        )
        for b in range(8)
    ]
    chunks = [
        pltpu.make_async_copy(
            mass_hbm.at[pl.ds(i * CHUNK, CHUNK)], raw.at[pl.ds(i * CHUNK, CHUNK)], msem.at[i]
        )
        for i in range(CHUNKS)
    ]
    locals_[4].start()
    locals_[5].start()
    for b in range(8):
        blocks[b].start()
    chunks[0].start()
    chunks[1].start()
    locals_[2].start()
    locals_[3].start()
    for i in range(2, CHUNKS):
        chunks[i].start()
    locals_[1].start()

    barrier = pltpu.get_barrier_semaphore()

    @pl.loop(1, ROWS)
    def _(d):
        pl.semaphore_signal(
            barrier, inc=1, device_id=(lax.rem(r + d, ROWS), c), device_id_type=MESH
        )

    @pl.loop(0, 4)
    def _(up):
        @pl.loop(1, COLS)
        def _(d):
            pl.semaphore_signal(
                barrier,
                inc=1,
                device_id=(lax.rem(z + up, 4) * 4 + x, lax.rem(c + d, COLS)),
                device_id_type=MESH,
            )

    for b in range(16):
        maskrow[:, b * TILE : (b + 1) * TILE] = jnp.broadcast_to(
            mask_ref[:, b : b + 1].astype(F32), (16, TILE)
        )

    def apply_mask(i):
        chunks[i].wait()
        for half in range(CHUNK // TILE):
            rows = i * CHUNK + half * TILE
            a = i * (CHUNK // TILE) + half
            m = jnp.broadcast_to(maskrow[a : a + 1, :], (16, N)).astype(BF16)
            for q in range(TILE // 16):
                masked[i, half * TILE + q * 16 : half * TILE + (q + 1) * 16, :] = (
                    raw[rows + q * 16 : rows + (q + 1) * 16, :] * m
                )

    for b in range(8):
        blocks[b].wait()
    for k in range(2):
        for i in range(4):
            at = 0
            for a in range(1, 4):
                at = at + a * is_block(map_ref[k, a], i)
            to = k * SEP + i * TILE
            cp[:, to : to + TILE] = cin[k * 4 + lax.rem(at, 4)]
    apply_mask(0)

    def row_copy(d, src, dst, send, recv):
        return pltpu.make_async_remote_copy(
            src_ref=src,
            dst_ref=dst,
            send_sem=send.at[d],
            recv_sem=recv.at[d],
            device_id=(lax.rem(r + d, ROWS), c),
            device_id_type=MESH,
        )

    def col_copy(d, src, dst, send, recv):
        return pltpu.make_async_remote_copy(
            src_ref=src,
            dst_ref=dst,
            send_sem=send.at[d],
            recv_sem=recv.at[d],
            device_id=(r, lax.rem(c + d, COLS)),
            device_id_type=MESH,
        )

    def each_row(fn):
        @pl.loop(1, ROWS)
        def _(d):
            fn(d)

    def each_col(fn):
        @pl.loop(1, COLS)
        def _(d):
            fn(d)

    def src_row(d):
        return lax.rem(r + ROWS - d, ROWS)

    def src_col(d):
        return lax.rem(c + COLS - d, COLS)

    def x_copy(d, m, at):
        return pltpu.make_async_remote_copy(
            src_ref=xall.at[r, m],
            dst_ref=xall.at[at, m],
            send_sem=x_send.at[m, d],
            recv_sem=x_recv.at[m, d],
            device_id=(lax.rem(r + d, ROWS), c),
            device_id_type=MESH,
        )

    def k_copy(d, at):
        s = lax.rem(slot + d, PLANE)
        return pltpu.make_async_remote_copy(
            src_ref=tcol.at[s],
            dst_ref=tcol_in.at[at],
            send_sem=k_send.at[d],
            recv_sem=k_recv.at[d],
            device_id=(lax.div(s, COLS) * 4 + x, lax.rem(s, COLS)),
            device_id_type=MESH,
        )
    def load_columns(i, m):
        cols = slice(m * SEP, (m + 1) * SEP)
        loaded[i * CHUNK : (i + 1) * CHUNK, cols] = dot_nn(masked[i], cp[:, cols]).astype(BF16)

    def basis(m):
        return xall[:, m].reshape(SEP, 128)

    def gram_of(matrix, m):
        x_high, x_low = split_two(basis(m))
        x_both = jnp.concatenate([x_high, x_low], axis=1)
        p_high, p_low = split_two(matrix)
        applied = dot_nn(p_high, x_both)
        applied = applied[:, 0:128] + applied[:, 128:256] + dot_nn(p_low, x_high)
        a_high, a_low = split_two(applied)
        term = dot_tn(x_both, a_high)
        gram[m] = term[0:128] + term[128:256] + dot_tn(x_high, a_low)

    def ring(phase, arr):
        along_z = (arr == 0) == (phase == 1)
        me = z if along_z else x

        def device(step):
            to = lax.rem(me + step + 4, 4)
            return (to * 4 + x, c) if along_z else (z * 4 + to, c)

        return me, device

    def source(phase, arr, dest, half):
        if phase == 1:
            if arr == 0:
                return pg.at[0, dest, pl.ds(half * 2, 2)]
            if arr == 2:
                return pg.at[1, pl.ds(half * 2, 2), dest]
            return pt.at[core, pl.ds(half * 2, 2), dest]
        return sg.at[arr // 2, dest, pl.ds(half * 16, 16)]

    boxes = {
        (1, 0): (opp1g, own1g, acc1g),
        (1, 1): (opp1t, own1t, acc1t),
        (2, 0): (opp2g, own2g, acc2g),
    }

    def box_of(phase, arr, kind, way):
        if arr == 1:
            return boxes[phase, 1][kind].at[way]
        return boxes[phase, 0][kind].at[arr // 2, way]

    def ring_copy(phase, arr, kind, way, src):
        _, device = ring(phase, arr)
        sem = ((phase - 1) * 3 + arr) * 6 + kind * 2 + way
        return pltpu.make_async_remote_copy(
            src_ref=src,
            dst_ref=box_of(phase, arr, kind, way),
            send_sem=r_send.at[sem],
            recv_sem=r_recv.at[sem],
            device_id=device(1 - 2 * way),
            device_id_type=MESH,
        )

    def opp_copy(phase, arr, way):
        me, _ = ring(phase, arr)
        return ring_copy(phase, arr, 0, way, source(phase, arr, lax.rem(me + 2, 4), way))

    def own_copy(phase, arr, way):
        me, _ = ring(phase, arr)
        dest = lax.rem(me + 1 - 2 * way + 4, 4)
        return ring_copy(phase, arr, 1, way, source(phase, arr, dest, 1 - way))

    def acc_copy(phase, arr, way):
        return ring_copy(phase, arr, 2, way, box_of(phase, arr, 0, way))

    def ring_start(phase, arrs, copy):
        for arr in arrs:
            for way in range(2):
                copy(phase, arr, way).start()

    def ring_pass(phase, arrs):
        for arr in arrs:
            me, _ = ring(phase, arr)
            for way in range(2):
                opp_copy(phase, arr, way).wait_recv()
                dest = lax.rem(me + 1 - 2 * way + 4, 4)
                box = box_of(phase, arr, 0, way)
                box[...] = box[...] + source(phase, arr, dest, way)[...]
                acc_copy(phase, arr, way).start()

    def ring_close(phase, arr):
        me, _ = ring(phase, arr)
        halves = []
        for half in range(2):
            acc_copy(phase, arr, half).wait_recv()
            own_copy(phase, arr, 1 - half).wait_recv()
            halves.append(
                source(phase, arr, me, half)[...]
                + box_of(phase, arr, 2, half)[...]
                + box_of(phase, arr, 1, 1 - half)[...]
            )
        return halves

    load_columns(0, 1)
    pl.semaphore_wait(barrier, ROWS - 1 + 4 * (COLS - 1))
    locals_[5].wait()
    each_row(lambda d: x_copy(d, 1, r).start())
    locals_[4].wait()
    each_row(lambda d: x_copy(d, 0, r).start())
    apply_mask(1)
    load_columns(1, 1)
    load_columns(0, 0)
    load_columns(1, 0)
    top = dot_tn(cp[:, SEP:], loaded[:, SEP:])
    for h in range(2):
        pt[h] = top[:, h * 256 : (h + 1) * 256].reshape(4, 4, 32, 256)
    locals_[3].wait()
    own_rows = lax.div(lax.broadcasted_iota(jnp.int32, (32, 256), 0), 4) == c
    own_top = jnp.concatenate([tmass[...]] * 8, axis=0)
    for h in range(2):
        pt[h, z, x] = pt[h, z, x] + jnp.where(own_rows, own_top[:, h * 256 : (h + 1) * 256], 0.0)
    swap = pltpu.make_async_remote_copy(
        src_ref=pt.at[1 - core],
        dst_ref=swapped,
        send_sem=w_sem.at[0],
        recv_sem=w_sem.at[1],
        device_id=(r, c + 1 - 2 * core),
        device_id_type=MESH,
    )
    swap.start()
    each_row(lambda d: x_copy(d, 1, src_row(d)).wait_recv())
    gram_of(
        jnp.concatenate([pt[0].reshape(SEP, 256), pt[1].reshape(SEP, 256)], axis=1), 1
    )
    for q in range(COLS):
        t_row[q] = gram[1, q * 16 : (q + 1) * 16, :]
    each_col(
        lambda d: col_copy(
            d, t_row.at[lax.rem(c + d, COLS)], t_in.at[c], ta_send, ta_recv
        ).start()
    )
    t_in[c] = t_row[c]
    swap.wait_recv()
    pt[core] = pt[core] + swapped[...]
    ring_start(1, (1,), opp_copy)

    group = dot_tn(cp[:, 0:SEP], loaded[:, 0:SEP])
    for h in range(2):
        pg[h] = group[:, h * 256 : (h + 1) * 256].reshape(4, 4, 32, 256)
    locals_[2].wait()
    for h in range(2):
        pg[h, z, x] = pg[h, z, x] + gmass[:, h * 256 : (h + 1) * 256]
    each_row(lambda d: x_copy(d, 0, src_row(d)).wait_recv())
    gram_of(
        jnp.concatenate([pg[0].reshape(SEP, 256), pg[1].reshape(SEP, 256)], axis=1), 0
    )
    for q in range(ROWS):
        g_sum[q] = gram[0, q * 8 : (q + 1) * 8, :]
    each_row(
        lambda d: row_copy(
            d, g_sum.at[lax.rem(r + d, ROWS)], g_in.at[r], g1_send, g1_recv
        ).start()
    )
    g_in[r] = g_sum[r]
    ring_start(1, (0, 2), opp_copy)

    locals_[1].wait()
    projected = dot_tn(fixed[...], loaded[...])
    for m in range(2):
        seen_ref[m] = dot_nn(
            projected[:, m * SEP : (m + 1) * SEP], basis(m), precision=HIGHEST
        )
    own_ref[...] = xall[r]

    each_col(
        lambda d: col_copy(d, t_row.at[0], t_in.at[src_col(d)], ta_send, ta_recv).wait_recv()
    )
    total = t_in[0]
    for q in range(1, COLS):
        total = total + t_in[q]
    t_sum[r] = total
    each_row(lambda d: row_copy(d, t_sum.at[r], t_sum.at[r], tb_send, tb_recv).start())
    ring_start(1, (1,), own_copy)
    ring_pass(1, (1,))

    each_row(
        lambda d: row_copy(d, g_sum.at[0], g_in.at[src_row(d)], g1_send, g1_recv).wait_recv()
    )
    total = g_in[0]
    for q in range(1, ROWS):
        total = total + g_in[q]
    g_all[r] = total
    each_row(lambda d: row_copy(d, g_all.at[r], g_all.at[r], g2_send, g2_recv).start())
    ring_start(1, (0, 2), own_copy)
    ring_pass(1, (0, 2))

    each_row(
        lambda d: row_copy(d, t_sum.at[r], t_sum.at[src_row(d)], tb_send, tb_recv).wait_recv()
    )
    total = t_sum[0]
    for q in range(1, ROWS):
        total = total + t_sum[q]
    t_all[c] = total
    each_col(lambda d: col_copy(d, t_all.at[c], t_all.at[c], tc_send, tc_recv).start())

    eye = (
        lax.broadcasted_iota(jnp.int32, (128, 128), 0)
        == lax.broadcasted_iota(jnp.int32, (128, 128), 1)
    ).astype(F32)

    def start_factor(m, whole):
        whole = whole.reshape(128, 128)
        ch[m, :, 0:128] = 0.5 * (whole + whole.T)
        ch[m, :, 128:256] = eye

    def panels(lo, hi):
        for p in range(lo, hi):
            factor_panel(ch, w_ref, p)

    halves = ring_close(1, 1)
    for half in range(2):
        for i in range(2):
            for q in range(COLS):
                tcol[(half * 2 + i) * COLS + q] = halves[half][i, q * 4 : (q + 1) * 4, :]

    @pl.loop(1, PLANE)
    def _(d):
        k_copy(d, slot).start()

    tcol_in[slot] = tcol[slot]
    for arr in (0, 2):
        halves = ring_close(1, arr)
        sg[arr // 2, 0:2] = halves[0]
        sg[arr // 2, 2:4] = halves[1]
    ring_start(2, (0, 2), opp_copy)
    ring_start(2, (0, 2), own_copy)

    each_row(
        lambda d: row_copy(d, g_all.at[r], g_all.at[src_row(d)], g2_send, g2_recv).wait_recv()
    )
    start_factor(0, g_all[...])
    each_col(
        lambda d: col_copy(d, t_all.at[c], t_all.at[src_col(d)], tc_send, tc_recv).wait_recv()
    )
    start_factor(1, t_all[...])

    panels(0, 8)
    ring_pass(2, (0, 2))
    panels(8, 16)
    for arr in (0, 2):
        halves = ring_close(2, arr)
        for half in range(2):
            gout_ref[half * 16 : (half + 1) * 16, arr * 128 : arr * 128 + 256] = SEP * halves[half]

    @pl.loop(1, PLANE)
    def _(d):
        k_copy(d, lax.rem(slot + PLANE - d, PLANE)).wait_recv()

    for h in range(2):
        total = tcol_in[h]
        for q in range(h + 2, PLANE, 2):
            total = total + tcol_in[q]
        apex_ref[:, h * 256 : (h + 1) * 256] = SEP * total

    def sends_row(d):
        x_copy(d, 0, r).wait_send()
        x_copy(d, 1, r).wait_send()
        row_copy(d, g_sum.at[0], g_in.at[r], g1_send, g1_recv).wait_send()
        row_copy(d, g_all.at[r], g_all.at[r], g2_send, g2_recv).wait_send()
        row_copy(d, t_sum.at[r], t_sum.at[r], tb_send, tb_recv).wait_send()

    def sends_col(d):
        col_copy(d, t_row.at[0], t_in.at[c], ta_send, ta_recv).wait_send()
        col_copy(d, t_all.at[c], t_all.at[c], tc_send, tc_recv).wait_send()

    swap.wait_send()
    each_row(sends_row)
    each_col(sends_col)

    @pl.loop(1, PLANE)
    def _(d):
        k_copy(d, slot).wait_send()

    for phase, arrs in ((1, (0, 1, 2)), (2, (0, 2))):
        for copy in (opp_copy, own_copy, acc_copy):
            for arr in arrs:
                for way in range(2):
                    copy(phase, arr, way).wait_send()


def finish(seen, inverse, own, gmatrix, tmatrix, coup, gmodes, tmodes, gout, apex):
    gout[...] = gmatrix[...]
    apex[...] = tmatrix[...]
    for m, modes in enumerate((gmodes, tmodes)):
        coup[:, m, :] = dot_nt(seen[m], inverse[m], precision=HIGHEST)
        modes[...] = dot_nt(own[m], inverse[m], precision=HIGHEST)


def body(
    leaf_mass,
    tile_mask,
    constraint_modes,
    leaf_fixed_modes,
    block_map,
    group_mass,
    top_mass,
    group_basis,
    top_basis,
):
    hbm = pl.BlockSpec(memory_space=pl.ANY)
    vmem = pl.BlockSpec(memory_space=pltpu.VMEM)
    smem = pl.BlockSpec(memory_space=pltpu.SMEM)
    dma = pltpu.SemaphoreType.DMA
    half1g = (2, 2, 2, 32, SEP // 2)
    half1t = (2, 2, 32, SEP // 2)
    half2g = (2, 2, 16, SEP // 2)
    scratch = [
        pltpu.VMEM((N, N), BF16),
        pltpu.VMEM((2, CHUNK, N), BF16),
        pltpu.VMEM((8, N, TILE), BF16),
        pltpu.VMEM((N, 2 * SEP), BF16),
        pltpu.VMEM((N, 2 * SEP), BF16),
        pltpu.VMEM((N, 128), BF16),
        pltpu.VMEM((16, N), F32),
        pltpu.VMEM((32, SEP), F32),
        pltpu.VMEM((4, SEP), F32),
        pltpu.VMEM((ROWS, 2, 32, 128), F32),
        pltpu.VMEM((2, 4, 4, 32, SEP // 2), F32),
        pltpu.VMEM((2, 4, 4, 32, SEP // 2), F32),
        pltpu.VMEM((4, 4, 32, SEP // 2), F32),
        pltpu.VMEM((2, 128, 128), F32),
        pltpu.VMEM((ROWS, 8, 128), F32),
        pltpu.VMEM((ROWS, 8, 128), F32),
        pltpu.VMEM((ROWS, 8, 128), F32),
        pltpu.VMEM((COLS, 16, 128), F32),
        pltpu.VMEM((ROWS, 16, 128), F32),
        pltpu.VMEM((COLS, 16, 128), F32),
        pltpu.VMEM((COLS, 16, 128), F32),
        pltpu.VMEM((COLS, 16, 128), F32),
        pltpu.VMEM(half1g, F32),
        pltpu.VMEM(half1g, F32),
        pltpu.VMEM(half1g, F32),
        pltpu.VMEM(half1t, F32),
        pltpu.VMEM(half1t, F32),
        pltpu.VMEM(half1t, F32),
        pltpu.VMEM((2, 4, 32, SEP // 2), F32),
        pltpu.VMEM(half2g, F32),
        pltpu.VMEM(half2g, F32),
        pltpu.VMEM(half2g, F32),
        pltpu.VMEM((PLANE, 4, SEP // 2), F32),
        pltpu.VMEM((PLANE, 4, SEP // 2), F32),
        pltpu.VMEM((2, 128, 256), F32),
        dma((6,)),
        dma((8,)),
        dma((CHUNKS,)),
        dma((2, ROWS)),
        dma((2, ROWS)),
        dma((ROWS,)),
        dma((ROWS,)),
        dma((ROWS,)),
        dma((ROWS,)),
        dma((COLS,)),
        dma((COLS,)),
        dma((ROWS,)),
        dma((ROWS,)),
        dma((COLS,)),
        dma((COLS,)),
        dma((36,)),
        dma((36,)),
        dma((PLANE,)),
        dma((PLANE,)),
        dma((2,)),
    ]
    seen, inverse, own, gout, apex = pl.pallas_call(
        kernel,
        out_shape=(
            jax.ShapeDtypeStruct((2, 128, 128), F32),
            jax.ShapeDtypeStruct((2, 128, 128), F32),
            jax.ShapeDtypeStruct((2, 32, 128), F32),
            jax.ShapeDtypeStruct((32, SEP), F32),
            jax.ShapeDtypeStruct((4, SEP), F32),
        ),
        in_specs=[hbm, vmem, hbm, hbm, smem, hbm, hbm, hbm, hbm],
        out_specs=(vmem, vmem, vmem, vmem, vmem),
        scratch_shapes=scratch,
        compiler_params=pltpu.CompilerParams(
            collective_id=0, has_side_effects=True, vmem_limit_bytes=60 << 20
        ),
        name="assemble",
    )(
        leaf_mass[0],
        tile_mask[0],
        constraint_modes[0],
        leaf_fixed_modes[0],
        block_map[0],
        group_mass[0],
        top_mass,
        group_basis[0],
        top_basis,
    )
    coupling, gmodes, tmodes, gout, apex = pl.pallas_call(
        finish,
        out_shape=(
            jax.ShapeDtypeStruct((128, 2, 128), F32),
            jax.ShapeDtypeStruct((32, 128), F32),
            jax.ShapeDtypeStruct((32, 128), F32),
            jax.ShapeDtypeStruct((32, SEP), F32),
            jax.ShapeDtypeStruct((4, SEP), F32),
        ),
        in_specs=[vmem] * 5,
        out_specs=(vmem,) * 5,
        name="finish",
    )(seen, inverse, own, gout, apex)
    return (coupling[None], gmodes[None], tmodes, gout[None], apex)


def solution(mesh):
    in_specs = (
        P(("row", "col"), None, None),
        P(("row", "col"), None, None),
        P(("row", "col"), None, None),
        P(("row", "col"), None, None),
        P(("row", "col"), None, None),
        P("col", "row", None),
        P(("row", "col"), None),
        P("col", "row", None),
        P("row", None),
    )
    out_specs = (
        P(("row", "col"), None, None, None),
        P("col", "row", None),
        P("row", None),
        P("col", "row", None),
        P(("row", "col"), None),
    )
    return jax.shard_map(body, mesh=mesh, in_specs=in_specs, out_specs=out_specs, check_vma=False)
```
